256 devices in a mesh: span: 4 (over x), seq: 64 (over y, z, core).
Axes of the slice: x: 4, y: 4, z: 8, core: 2. Of those that a mesh axis runs over, the one named last changes fastest.
Arguments:
- query_rows: bfloat16 [4, 14336, 3072], P('span', 'seq'), may hold values from -10 to 10
- key_rows: bfloat16 [4, 14336, 512], P('span', 'seq'), may hold values from -10 to 10
- value_rows: bfloat16 [4, 14336, 512], P('span', 'seq'), may hold values from -6 to 6
- owner_ids: int32 [4, 14336], P('span', 'seq'), may hold values from 0 to 63, as said below
Outputs:
- attended: bfloat16 [4, 14336, 3072], P('span', 'seq')
The draws below stay inside these ranges and needn't reach their ends.
Inputs may be any that keep to these rules, and one draw needn't show every extreme that they name: `owner_ids`: from the rows of one device at most 7 go to any one owner; in every time span one owner receives exactly 7 rows from every device of its span, and no owner more than 448 rows in all.
All inputs are finite; a program needn't handle non-finite values.
Results may differ from the reference program's by a relative error of at most 0.0055.
Values may be sent and summed in bfloat16 or wider, within the bound.
No kernel may reach another device: no remote copies, remote signals or barrier semaphores. Data moves between devices by JAX's collectives and lax.ppermute only.
A program may use at most 128 MiB of HBM per device.

```python
import math
import jax
import jax.numpy as jnp
from jax import lax

HQ = 24
KVH = 4
HD = 128
LOAD = 224
OWNERS = 64
GROUPS = 4
GROUP_ROWS = 14336
OWN = 448


def drawn_rows(key, salt_value, row_width):
    full_shape = (GROUPS, GROUP_ROWS, row_width)
    drawn = jax.random.normal(jax.random.fold_in(key, salt_value), full_shape, jnp.float32)
    return jnp.clip(drawn, -10.0, 10.0)


def draw_query_rows(key, part):
    return drawn_rows(key, 101, HQ * HD).astype(jnp.bfloat16)


def draw_key_rows(key, part):
    return drawn_rows(key, 202, KVH * HD).astype(jnp.bfloat16)


def draw_owner_ids(key, part):

    def one_group(group):
        group_key = jax.random.fold_in(jax.random.fold_in(key, 303), group)
        busiest = jax.random.randint(jax.random.fold_in(group_key, 1), (), 0, OWNERS)
        owner_index = jnp.arange(OWNERS, dtype=jnp.int32)
        shares = jax.random.randint(jax.random.fold_in(group_key, 2), (OWNERS,), 2, 4)
        shares = jnp.where(owner_index == busiest, 0, shares)
        remaining = (OWNERS - 2) * LOAD
        base_counts = shares * remaining // jnp.sum(shares)
        leftover = remaining - jnp.sum(base_counts)
        nonbusy_rank = jnp.cumsum((shares > 0).astype(jnp.int32)) - 1
        counts = base_counts + jnp.where((shares > 0) & (nonbusy_rank < leftover), 1, 0)
        counts = jnp.where(owner_index == busiest, 2 * LOAD, counts)
        range_ends = jnp.cumsum(counts)
        position = jnp.arange(LOAD, dtype=jnp.int32)[None, :] * OWNERS + owner_index[:, None]
        owner_of = jnp.sum((position[:, :, None] >= range_ends[None, None, :]).astype(jnp.int32), axis=2)
        shuffle = jax.vmap(lambda sub_key: jax.random.permutation(sub_key, LOAD))(jax.random.split(jax.random.fold_in(group_key, 3), OWNERS))
        return jnp.take_along_axis(owner_of, shuffle, axis=1).reshape(GROUP_ROWS).astype(jnp.int32)
    return jax.vmap(one_group)(jnp.arange(GROUPS, dtype=jnp.int32))


def level_of(rng, extent, pieces, smallest, high):
    def one(dim, blocks):
        heights = jax.random.uniform(jax.random.fold_in(jax.random.fold_in(rng, 6), dim), (blocks,), jnp.float32, smallest / len(pieces), high / len(pieces))
        return jnp.repeat(jnp.exp(heights), extent[dim] // blocks).reshape((-1,) + (1,) * (len(extent) - dim - 1))

    level = one(*pieces[0])
    for cut in pieces[1:]:
        level = level * one(*cut)
    return level


def scatter_about(own_key, extent, width, limit, shards=(), kind=jnp.bfloat16):
    array = width * jax.random.normal(own_key, extent, jnp.float32)
    if shards:
        array = array * level_of(own_key, extent, shards, -0.22, 0.18)
    return jnp.clip(array, -limit, limit).astype(kind)


def setup_inputs(seed: int = 0) -> dict:
    key_of = jax.random.split(jax.random.key(seed), 5)
    return {
        "query_rows": draw_query_rows(jax.random.fold_in(key_of[4], 71), 0),
        "key_rows": draw_key_rows(jax.random.fold_in(key_of[4], 71), 0),
        "value_rows": scatter_about(key_of[2], (GROUPS, GROUP_ROWS, KVH * HD), 1.0, 6.0, ((0, 4), (1, 64))),
        "owner_ids": draw_owner_ids(jax.random.fold_in(key_of[4], 71), 0),
    }


def attend_owner(query_pad, key_pad, value_pad, tag_pad):
    total = query_pad.shape[0]
    span_of = jnp.arange(total, dtype=jnp.int32) // OWN
    allowed = (tag_pad[None, :] == tag_pad[:, None]) & (span_of[None, :] <= span_of[:, None])
    group_size = HQ // KVH
    query_heads = query_pad.astype(jnp.float32).reshape(total, KVH, group_size, HD).transpose(1, 0, 2, 3)
    key_heads = key_pad.astype(jnp.float32).reshape(total, KVH, HD).transpose(1, 0, 2)
    value_heads = value_pad.astype(jnp.float32).reshape(total, KVH, HD).transpose(1, 0, 2)

    def per_group(slices):
        query_group, key_group, value_group = slices
        scores = jnp.einsum('qhd,kd->hqk', query_group, key_group) / math.sqrt(HD)
        scores = jnp.where(allowed[None], scores, jnp.float32(-1e+30))
        row_max = lax.optimization_barrier(jnp.max(scores, axis=-1))
        weights = jnp.where(allowed[None], jnp.exp(scores - row_max[..., None]), jnp.float32(0.0))
        row_total = lax.optimization_barrier(jnp.sum(weights, axis=-1))
        rounded = weights.astype(jnp.bfloat16).astype(jnp.float32)
        numer = jnp.einsum('hqk,kd->hqd', rounded, value_group)
        return numer / row_total[..., None]
    result = lax.map(per_group, (query_heads, key_heads, value_heads))
    return result.transpose(2, 0, 1, 3).reshape(total, HQ * HD).astype(jnp.bfloat16)

def reference(query_rows, key_rows, value_rows, owner_ids):
    owner_index = jnp.arange(OWNERS, dtype=jnp.int32)
    owner_hits = (owner_ids[..., None] == owner_index).astype(jnp.int32)
    slot_rank = lax.optimization_barrier(jnp.sum(jnp.cumsum(owner_hits, axis=1) * owner_hits, axis=2)) - 1
    group_index = jnp.arange(GROUPS, dtype=jnp.int32)[:, None]
    flat_slot = ((owner_ids * GROUPS + group_index) * OWN + slot_rank).astype(jnp.int32).reshape(-1)
    slab_rows = OWNERS * GROUPS * OWN
    query_pad = jnp.zeros((slab_rows, HQ * HD), jnp.bfloat16).at[flat_slot].set(query_rows.reshape(-1, HQ * HD))
    key_pad = jnp.zeros((slab_rows, KVH * HD), jnp.bfloat16).at[flat_slot].set(key_rows.reshape(-1, KVH * HD))
    value_pad = jnp.zeros((slab_rows, KVH * HD), jnp.bfloat16).at[flat_slot].set(value_rows.reshape(-1, KVH * HD))
    tag_pad = jnp.zeros((slab_rows,), jnp.int32).at[flat_slot].set(jnp.ones((flat_slot.shape[0],), jnp.int32))
    query_pad = query_pad.reshape(OWNERS, GROUPS * OWN, HQ * HD)
    key_pad = key_pad.reshape(OWNERS, GROUPS * OWN, KVH * HD)
    value_pad = value_pad.reshape(OWNERS, GROUPS * OWN, KVH * HD)
    tag_pad = tag_pad.reshape(OWNERS, GROUPS * OWN)
    output_pad = lax.map(lambda slices: attend_owner(slices[0], slices[1], slices[2], slices[3]), (query_pad, key_pad, value_pad, tag_pad))
    output_flat = output_pad.reshape(slab_rows, HQ * HD)
    return output_flat[flat_slot].reshape(GROUPS, GROUP_ROWS, HQ * HD)
```

```python
import functools
import math

import jax
import jax.numpy as jnp
from jax import lax
from jax.experimental import pallas as pl
from jax.experimental.pallas import tpu as pltpu
from jax.sharding import PartitionSpec as P

HQ = 24
KVH = 4
HD = 128
GROUP = HQ // KVH
TILE = 8
SLOTS = 7
CHUNK_HEADS = 8
CHUNKS = HQ // CHUNK_HEADS
WIDE = SLOTS * HD
KEY_BLOCK = 224
QUERY_BLOCK = 64
F32 = jnp.float32
BF16 = jnp.bfloat16
VMEM_LIMIT = 44 << 20


def iota(shape, dim):
    return lax.broadcasted_iota(jnp.int32, shape, dim)


def row_ranks(owner_ref):
    count = owner_ref.shape[1]
    along = jnp.broadcast_to(owner_ref[...].astype(F32), (count, count))
    down = along.T
    earlier = (along == down) & (iota((count, count), 0) < iota((count, count), 1))
    rank = jnp.sum(jnp.where(earlier, 1.0, 0.0), axis=0, keepdims=True)
    return owner_ref[...], rank.astype(jnp.int32)


def row_ranks_down(owner_ref):
    count = owner_ref.shape[1]
    along = jnp.broadcast_to(owner_ref[...].astype(F32), (count, count))
    down = along.T
    earlier = (along == down) & (iota((count, count), 1) < iota((count, count), 0))
    rank = jnp.sum(jnp.where(earlier, 1.0, 0.0), axis=1, keepdims=True)
    return down[:, :1].astype(jnp.int32), rank.astype(jnp.int32)


def one_hot(condition):
    return jnp.where(condition, 1.0, 0.0).astype(BF16)


def pack_kv_kernel(owner_ref, key_ref, value_ref, out_ref):
    owner, rank = row_ranks(owner_ref)
    count = owner.shape[1]
    rows = out_ref.shape[0]
    place = iota((rows, count), 0)
    select = one_hot(place == owner * TILE + rank)
    hits = jnp.sum(jnp.where(place == owner * TILE + SLOTS, 1.0, 0.0), axis=1, keepdims=True)
    half = KVH * HD
    keys = jnp.dot(select, key_ref[...], preferred_element_type=F32)
    out_ref[:, :half] = (keys + hits).astype(BF16)
    values = jnp.dot(select, value_ref[...], preferred_element_type=F32)
    out_ref[:, half:] = (values + hits).astype(BF16)


def pack_q_kernel(owner_ref, query_ref, *out_refs):
    owner, rank = row_ranks(owner_ref)
    count = owner.shape[1]
    rows = out_refs[0].shape[0]
    place = iota((rows, count), 0)
    select = one_hot(place == owner * TILE + rank)
    spare = place == owner * TILE + SLOTS
    last = CHUNK_HEADS - 1
    tails = jnp.concatenate(
        [query_ref[:, (c * CHUNK_HEADS + last) * HD : (c + 1) * CHUNK_HEADS * HD] for c in range(CHUNKS)],
        axis=1,
    )
    for c in range(CHUNKS):
        first = c * CHUNK_HEADS * HD
        moved = jnp.dot(select, query_ref[:, first : first + WIDE], preferred_element_type=F32)
        out_refs[c][...] = moved.astype(BF16)
    for k in range(SLOTS):
        moved = jnp.dot(one_hot(spare & (rank == k)), tails, preferred_element_type=F32).astype(BF16)
        for c in range(CHUNKS):
            out_refs[c][:, k * HD : (k + 1) * HD] += moved[:, c * HD : (c + 1) * HD]


def compact_kernel(got_ref, kv_ref, fold_ref, unfold_ref):
    rows = got_ref.shape[0]
    own_rows = fold_ref.shape[0]
    counts = got_ref[:, :HD].astype(F32).T[:TILE].astype(BF16)
    source = iota((rows, rows), 0)
    target = iota((rows, rows), 1)
    spare = (source & (TILE - 1)) == SLOTS
    base = target - (target & (TILE - 1))
    before = one_hot(spare & (source < base))
    same = one_hot(source == base + SLOTS)
    offset = jnp.dot(counts, before, preferred_element_type=F32)[:1].astype(jnp.int32)
    held = jnp.dot(counts, same, preferred_element_type=F32)[:1].astype(jnp.int32)
    slot = iota((1, rows), 1) & (TILE - 1)
    place = jnp.where(slot < held, offset + slot, -1)
    fold = jnp.where(iota((own_rows, rows), 0) == place, 1.0, 0.0)
    fold_ref[...] = fold.astype(BF16)
    unfold_ref[...] = fold.T.astype(BF16)
    moved = jnp.dot(fold.astype(BF16), got_ref[...], preferred_element_type=F32)
    kv_ref[:own_rows, :] = moved.astype(BF16)
    total = jnp.sum(jnp.where(slot == SLOTS, held, 0), axis=1, keepdims=True)
    wide = kv_ref.shape[1]
    lane = iota((TILE, wide), 1)
    kv_ref[own_rows:, :] = jnp.where(lane < HD, total >> 3, total & 7).astype(F32).astype(BF16)


def spread_tail(rows_f32):
    tiles = rows_f32.shape[0] // TILE
    view = rows_f32.reshape(tiles, TILE, rows_f32.shape[1])
    sub = iota((tiles, TILE, HD), 1)
    tail = jnp.zeros((tiles, TILE, HD), F32)
    for k in range(SLOTS):
        piece = jnp.broadcast_to(view[:, SLOTS:, k * HD : (k + 1) * HD], (tiles, TILE, HD))
        tail = jnp.where(sub == k, piece, tail)
    return tail.reshape(tiles * TILE, HD)


def attend_kernel(chunk, got_ref, kv_ref, fold_ref, unfold_ref, out_ref, x_ref, held_ref, count_ref):
    rows = got_ref.shape[0]
    own_rows = fold_ref.shape[0]
    spans = kv_ref.shape[0]
    span_now = lax.axis_index("span")
    factor = F32(math.log2(math.e) / math.sqrt(HD))
    x_ref[:, :WIDE] = got_ref[...]
    x_ref[:, WIDE:] = spread_tail(got_ref[...].astype(F32)).astype(BF16)
    held_ref[...] = jnp.zeros_like(held_ref)
    query_count = jnp.int32(0)
    for t in range(spans):
        note = kv_ref[t, own_rows:, : 2 * HD].astype(F32)
        high = jnp.max(note[:, :HD]).astype(jnp.int32)
        low = jnp.max(note[:, HD:]).astype(jnp.int32)
        total = high * 8 + low
        count_ref[t] = total
        query_count = jnp.where(span_now == t, total, query_count)
    heads = [chunk * CHUNK_HEADS + j for j in range(CHUNK_HEADS)]
    groups = []
    for kv_head in range(KVH):
        members = [j for j, h in enumerate(heads) if h // GROUP == kv_head]
        if members:
            groups.append((kv_head, members))

    def query_step(block, _):
        at = pl.ds(pl.multiple_of(block * QUERY_BLOCK, QUERY_BLOCK), QUERY_BLOCK)
        query = jnp.dot(fold_ref[at, :], x_ref[...], preferred_element_type=F32).astype(BF16)
        stacked = [
            jnp.concatenate([query[:, j * HD : (j + 1) * HD] for j in members], axis=0)
            for _, members in groups
        ]

        def span_step(t, carry):
            keys_here = count_ref[t]

            def key_step(b, carry):
                lower = pl.multiple_of(b * KEY_BLOCK, KEY_BLOCK)
                keys_at = pl.ds(lower, KEY_BLOCK)
                out = []
                for (kv_head, members), stack, (top, total, accum) in zip(groups, stacked, carry):
                    key = kv_ref[t, keys_at, kv_head * HD : (kv_head + 1) * HD]
                    value = kv_ref[t, keys_at, (KVH + kv_head) * HD : (KVH + kv_head + 1) * HD]
                    scores = lax.dot_general(
                        stack, key, (((1,), (1,)), ((), ())), preferred_element_type=F32
                    )
                    seen = iota(scores.shape, 1) < keys_here - lower
                    scores = jnp.where(seen, scores * factor, F32(-1e30))
                    new_top = jnp.maximum(top, jnp.max(scores, axis=1, keepdims=True))
                    weights = jnp.exp2(scores - new_top)
                    rescale = jnp.exp2(top - new_top)
                    new_total = rescale * total + jnp.sum(weights, axis=1, keepdims=True)
                    new_accum = rescale * accum + jnp.dot(
                        weights.astype(BF16), value, preferred_element_type=F32
                    )
                    out.append((new_top, new_total, new_accum))
                return tuple(out)

            return lax.fori_loop(0, (keys_here + KEY_BLOCK - 1) // KEY_BLOCK, key_step, carry)

        start = tuple(
            (
                jnp.full((stack.shape[0], 1), -1e30, F32),
                jnp.zeros((stack.shape[0], 1), F32),
                jnp.zeros((stack.shape[0], HD), F32),
            )
            for stack in stacked
        )
        final = lax.fori_loop(0, span_now + 1, span_step, start)
        for (_, members), (_, total, accum) in zip(groups, final):
            result = (accum / total).astype(BF16)
            for i, j in enumerate(members):
                held_ref[at, j * HD : (j + 1) * HD] = result[i * QUERY_BLOCK : (i + 1) * QUERY_BLOCK]
        return 0

    lax.fori_loop(0, (query_count + QUERY_BLOCK - 1) // QUERY_BLOCK, query_step, 0)
    moved = jnp.dot(unfold_ref[...], held_ref[...], preferred_element_type=F32)
    tiles = rows // TILE
    view = moved.reshape(tiles, TILE, CHUNK_HEADS * HD)
    sub = iota((tiles, TILE, HD), 1)
    tail = view[:, :, WIDE:]
    for k in range(SLOTS):
        piece = jnp.broadcast_to(tail[:, k : k + 1, :], (tiles, TILE, HD))
        whole = jnp.where(sub == SLOTS, piece, view[:, :, k * HD : (k + 1) * HD])
        out_ref[:, k * HD : (k + 1) * HD] = whole.reshape(rows, HD).astype(BF16)


def unpack_kernel(owner_ref, *refs):
    got_refs, out_ref = refs[:-1], refs[-1]
    owner, rank = row_ranks_down(owner_ref)
    count = owner.shape[0]
    rows = got_refs[0].shape[0]
    pick = one_hot(iota((count, rows), 1) == owner * TILE + rank)
    for c, got_ref in enumerate(got_refs):
        first = c * CHUNK_HEADS * HD
        main = jnp.dot(pick, got_ref[...], preferred_element_type=F32)
        out_ref[:, first : first + WIDE] = main.astype(BF16)
        tail = spread_tail(got_ref[...].astype(F32)).astype(BF16)
        last = jnp.dot(pick, tail, preferred_element_type=F32)
        out_ref[:, first + WIDE : first + CHUNK_HEADS * HD] = last.astype(BF16)


def call(kernel, name, out_shape, flops, moved, scratch=()):
    return pl.pallas_call(
        kernel,
        out_shape=out_shape,
        scratch_shapes=list(scratch),
        compiler_params=pltpu.CompilerParams(vmem_limit_bytes=VMEM_LIMIT),
        cost_estimate=pl.CostEstimate(flops=flops, bytes_accessed=moved, transcendentals=0),
        name=name,
    )


def exchange(rows, owners):
    shaped = rows.reshape(owners, TILE, rows.shape[1])
    return lax.all_to_all(shaped, "seq", split_axis=0, concat_axis=0, tiled=True).reshape(rows.shape)


def local(query_rows, key_rows, value_rows, owner_ids):
    owners = lax.axis_size("seq")
    spans = lax.axis_size("span")
    row_count = query_rows.shape[1]
    rows = owners * TILE
    own_rows = owners * SLOTS
    half = KVH * HD
    shape = jax.ShapeDtypeStruct

    send_kv = call(
        pack_kv_kernel, "pack_kv", shape((rows, 2 * half), BF16), rows * row_count * 4 * half, 4 * rows * half
    )(owner_ids, key_rows[0], value_rows[0])
    send_q = call(
        pack_q_kernel,
        "pack_q",
        [shape((rows, WIDE), BF16)] * CHUNKS,
        4 * rows * row_count * HQ * HD,
        4 * rows * HQ * HD,
    )(owner_ids, query_rows[0])
    got_kv = exchange(send_kv, owners)
    got_q = [exchange(part, owners) for part in send_q]
    own_kv, fold, unfold = call(
        compact_kernel,
        "compact",
        [
            shape((own_rows + TILE, 2 * half), BF16),
            shape((own_rows, rows), BF16),
            shape((rows, own_rows), BF16),
        ],
        2 * own_rows * rows * 2 * half,
        8 * rows * half,
    )(got_kv)
    all_kv = lax.all_gather(own_kv, "span", axis=0)
    got_out = []
    for chunk in range(CHUNKS):
        done = call(
            functools.partial(attend_kernel, chunk),
            "attend",
            shape((rows, WIDE), BF16),
            4 * own_rows * own_rows * spans * HD * CHUNK_HEADS,
            8 * rows * WIDE,
            [
                pltpu.VMEM((rows, CHUNK_HEADS * HD), BF16),
                pltpu.VMEM((own_rows, CHUNK_HEADS * HD), BF16),
                pltpu.SMEM((spans,), jnp.int32),
            ],
        )(got_q[chunk], all_kv, fold, unfold)
        got_out.append(exchange(done, owners))
    result = call(
        unpack_kernel,
        "unpack",
        shape((row_count, HQ * HD), BF16),
        4 * rows * row_count * HQ * HD,
        4 * rows * HQ * HD,
    )(owner_ids, *got_out)
    return result[None]


def solution(mesh):
    return jax.shard_map(
        local,
        mesh=mesh,
        in_specs=(
            P("span", "seq", None),
            P("span", "seq", None),
            P("span", "seq", None),
            P("span", "seq"),
        ),
        out_specs=P("span", "seq", None),
        check_vma=False,
    )
```

```python
import math

import jax
import jax.numpy as jnp
from jax import lax
from jax.experimental import pallas as pl
from jax.experimental.pallas import tpu as pltpu
from jax.sharding import PartitionSpec as P

HQ = 24
KVH = 4
HD = 128
GROUP = HQ // KVH
TILE = 8
SLOTS = 7
CHUNK_HEADS = 8
CHUNKS = HQ // CHUNK_HEADS
WIDE = SLOTS * HD
KEY_BLOCK = 256
QUERY_BLOCK = 64
COPY_BLOCK = 64
ALIGN = 16
PAIR = 2
F32 = jnp.float32
BF16 = jnp.bfloat16
VMEM_LIMIT = 44 << 20


def iota(shape, dim):
    return lax.broadcasted_iota(jnp.int32, shape, dim)


def row_ranks(owner_ref):
    count = owner_ref.shape[1]
    along = jnp.broadcast_to(owner_ref[...].astype(F32), (count, count))
    down = along.T
    earlier = (along == down) & (iota((count, count), 0) < iota((count, count), 1))
    rank = jnp.sum(jnp.where(earlier, 1.0, 0.0), axis=0, keepdims=True)
    return owner_ref[...], rank.astype(jnp.int32)


def row_ranks_down(owner_ref):
    count = owner_ref.shape[1]
    along = jnp.broadcast_to(owner_ref[...].astype(F32), (count, count))
    down = along.T
    earlier = (along == down) & (iota((count, count), 1) < iota((count, count), 0))
    rank = jnp.sum(jnp.where(earlier, 1.0, 0.0), axis=1, keepdims=True)
    return down[:, :1].astype(jnp.int32), rank.astype(jnp.int32)


def one_hot(condition):
    return jnp.where(condition, 1.0, 0.0).astype(BF16)


def pack_kv_kernel(owner_ref, key_ref, value_ref, out_ref):
    owner, rank = row_ranks(owner_ref)
    count = owner.shape[1]
    rows = out_ref.shape[0]
    place = iota((rows, count), 0)
    select = one_hot(place == owner * TILE + rank)
    hits = jnp.sum(jnp.where(place == owner * TILE + SLOTS, 1.0, 0.0), axis=1, keepdims=True)
    half = KVH * HD
    keys = jnp.dot(select, key_ref[...], preferred_element_type=F32)
    out_ref[:, :half] = (keys + hits).astype(BF16)
    values = jnp.dot(select, value_ref[...], preferred_element_type=F32)
    out_ref[:, half:] = (values + hits).astype(BF16)


def pack_q_kernel(owner_ref, query_ref, out_ref):
    owner, rank = row_ranks(owner_ref)
    count = owner.shape[1]
    rows = out_ref.shape[0]
    place = iota((rows, count), 0)
    select = one_hot(place == owner * TILE + rank)
    spare = place == owner * TILE + SLOTS
    last = CHUNK_HEADS - 1
    tails = jnp.concatenate(
        [query_ref[:, (c * CHUNK_HEADS + last) * HD : (c + 1) * CHUNK_HEADS * HD] for c in range(CHUNKS)],
        axis=1,
    )
    for c in range(CHUNKS):
        first = c * CHUNK_HEADS * HD
        moved = jnp.dot(select, query_ref[:, first : first + WIDE], preferred_element_type=F32)
        out_ref[:, c * WIDE : (c + 1) * WIDE] = moved.astype(BF16)
    for k in range(SLOTS):
        moved = jnp.dot(one_hot(spare & (rank == k)), tails, preferred_element_type=F32).astype(BF16)
        for c in range(CHUNKS):
            first = c * WIDE + k * HD
            out_ref[:, first : first + HD] += moved[:, c * HD : (c + 1) * HD]


def compact_kernel(got_ref, kv_ref, fold_ref, unfold_ref):
    rows = got_ref.shape[0]
    own_rows = fold_ref.shape[0]
    counts = got_ref[:, :HD].astype(F32).T[:TILE].astype(BF16)
    source = iota((rows, rows), 0)
    target = iota((rows, rows), 1)
    spare = (source & (TILE - 1)) == SLOTS
    base = target - (target & (TILE - 1))
    before = one_hot(spare & (source < base))
    same = one_hot(source == base + SLOTS)
    offset = jnp.dot(counts, before, preferred_element_type=F32)[:1].astype(jnp.int32)
    held = jnp.dot(counts, same, preferred_element_type=F32)[:1].astype(jnp.int32)
    slot = iota((1, rows), 1) & (TILE - 1)
    place = jnp.where(slot < held, offset + slot, -1)
    fold = jnp.where(iota((own_rows, rows), 0) == place, 1.0, 0.0)
    fold_ref[...] = fold.astype(BF16)
    unfold_ref[...] = fold.T.astype(BF16)
    moved = jnp.dot(fold.astype(BF16), got_ref[...], preferred_element_type=F32)
    kv_ref[:own_rows, :] = moved.astype(BF16)
    total = jnp.sum(jnp.where(slot == SLOTS, held, 0), axis=1, keepdims=True)
    wide = kv_ref.shape[1]
    lane = iota((TILE, wide), 1)
    kv_ref[own_rows:, :] = jnp.where(lane < HD, total >> 3, total & 7).astype(F32).astype(BF16)


def spread_tail(rows_f32):
    tiles = rows_f32.shape[0] // TILE
    view = rows_f32.reshape(tiles, TILE, rows_f32.shape[1])
    sub = iota((tiles, TILE, HD), 1)
    tail = jnp.zeros((tiles, TILE, HD), F32)
    for k in range(SLOTS):
        piece = jnp.broadcast_to(view[:, SLOTS:, k * HD : (k + 1) * HD], (tiles, TILE, HD))
        tail = jnp.where(sub == k, piece, tail)
    return tail.reshape(tiles * TILE, HD)


def attend_kernel(
    got_ref, kv_ref, fold_ref, unfold_ref, out_ref, x_ref, held_ref, k_ref, v_ref, turned_ref, bias_ref, count_ref
):
    rows = got_ref.shape[0]
    own_rows = fold_ref.shape[0]
    spans = kv_ref.shape[0]
    half = KVH * HD
    span_now = lax.axis_index("span")
    factor = F32(math.log2(math.e) / math.sqrt(HD))
    wide = CHUNK_HEADS * HD
    for c in range(CHUNKS):
        part = got_ref[:, c * WIDE : (c + 1) * WIDE]
        x_ref[:, c * wide : c * wide + WIDE] = part
        x_ref[:, c * wide + WIDE : (c + 1) * wide] = spread_tail(part.astype(F32)).astype(BF16)
    held_ref[...] = jnp.zeros_like(held_ref)
    k_ref[...] = jnp.zeros_like(k_ref)
    v_ref[...] = jnp.zeros_like(v_ref)
    bias_ref[...] = jnp.full(bias_ref.shape, -1e30, F32)
    query_count = jnp.int32(0)
    for t in range(spans):
        note = kv_ref[t, own_rows:, : 2 * HD].astype(F32)
        high = jnp.max(note[:, :HD]).astype(jnp.int32)
        low = jnp.max(note[:, HD:]).astype(jnp.int32)
        total = high * 8 + low
        count_ref[t] = total
        query_count = jnp.where(span_now == t, total, query_count)

    def copy_span(t, offset):
        here = count_ref[t]

        def copy_block(i, _):
            source = pl.ds(pl.multiple_of(i * COPY_BLOCK, COPY_BLOCK), COPY_BLOCK)
            target = pl.ds(pl.multiple_of(offset + i * COPY_BLOCK, ALIGN), COPY_BLOCK)
            k_ref[target, :] = kv_ref[t, source, :half]
            v_ref[target, :] = kv_ref[t, source, half:]
            valid = iota((COPY_BLOCK, HD), 0) + i * COPY_BLOCK < here
            bias_ref[target, :] = jnp.where(valid, F32(0.0), F32(-1e30))
            return 0

        lax.fori_loop(0, (here + COPY_BLOCK - 1) // COPY_BLOCK, copy_block, 0)
        return offset + (here + ALIGN - 1) // ALIGN * ALIGN

    key_count = lax.fori_loop(0, span_now + 1, copy_span, jnp.int32(0))
    key_blocks = (key_count + KEY_BLOCK - 1) // KEY_BLOCK

    def turn_block(b, _):
        at = pl.ds(pl.multiple_of(b * KEY_BLOCK, KEY_BLOCK), KEY_BLOCK)
        turned_ref[b] = v_ref[at, :].astype(F32).T.astype(BF16)
        return 0

    lax.fori_loop(0, key_blocks, turn_block, 0)
    lanes = GROUP * QUERY_BLOCK

    def query_step(block, _):
        at = pl.ds(pl.multiple_of(block * QUERY_BLOCK, QUERY_BLOCK), QUERY_BLOCK)
        for pair in range(0, KVH, PAIR):
            members = range(pair, pair + PAIR)
            turned_queries = []
            for kv_head in members:
                first = kv_head * GROUP * HD
                query = jnp.dot(
                    fold_ref[at, :], x_ref[:, first : first + GROUP * HD], preferred_element_type=F32
                )
                stack = jnp.concatenate([query[:, i * HD : (i + 1) * HD] for i in range(GROUP)], axis=0)
                turned_queries.append(stack.T.astype(BF16))

            def key_step(b, carry):
                keys_at = pl.ds(pl.multiple_of(b * KEY_BLOCK, KEY_BLOCK), KEY_BLOCK)
                bias = jnp.concatenate([bias_ref[keys_at, :]] * (lanes // HD), axis=1)
                out = []
                for kv_head, query, (top, total, accum) in zip(members, turned_queries, carry):
                    own = slice(kv_head * HD, (kv_head + 1) * HD)
                    scores = jnp.dot(k_ref[keys_at, own], query, preferred_element_type=F32)
                    scores = scores * factor + bias
                    new_top = jnp.maximum(top, jnp.max(scores, axis=0, keepdims=True))
                    weights = jnp.exp2(scores - new_top)
                    rescale = jnp.exp2(top - new_top)
                    new_total = rescale * total + jnp.sum(weights, axis=0, keepdims=True)
                    new_accum = rescale * accum + jnp.dot(
                        turned_ref[b, own, :], weights.astype(BF16), preferred_element_type=F32
                    )
                    out.append((new_top, new_total, new_accum))
                return tuple(out)

            start = (
                jnp.full((1, lanes), -1e30, F32),
                jnp.zeros((1, lanes), F32),
                jnp.zeros((HD, lanes), F32),
            )
            final = lax.fori_loop(0, key_blocks, key_step, (start,) * PAIR)
            for kv_head, (_, total, accum) in zip(members, final):
                result = (accum / total).T.astype(BF16)
                for i in range(GROUP):
                    head = kv_head * GROUP + i
                    held_ref[at, head * HD : (head + 1) * HD] = result[i * QUERY_BLOCK : (i + 1) * QUERY_BLOCK]
        return 0

    lax.fori_loop(0, (query_count + QUERY_BLOCK - 1) // QUERY_BLOCK, query_step, 0)
    tiles = rows // TILE
    sub = iota((tiles, TILE, HD), 1)
    for c in range(CHUNKS):
        moved = jnp.dot(unfold_ref[...], held_ref[:, c * wide : (c + 1) * wide], preferred_element_type=F32)
        view = moved.reshape(tiles, TILE, wide)
        tail = view[:, :, WIDE:]
        for k in range(SLOTS):
            piece = jnp.broadcast_to(tail[:, k : k + 1, :], (tiles, TILE, HD))
            whole = jnp.where(sub == SLOTS, piece, view[:, :, k * HD : (k + 1) * HD])
            first = c * WIDE + k * HD
            out_ref[:, first : first + HD] = whole.reshape(rows, HD).astype(BF16)


def unpack_kernel(owner_ref, got_ref, out_ref):
    owner, rank = row_ranks_down(owner_ref)
    count = owner.shape[0]
    rows = got_ref.shape[0]
    pick = one_hot(iota((count, rows), 1) == owner * TILE + rank)
    for c in range(CHUNKS):
        first = c * CHUNK_HEADS * HD
        part = got_ref[:, c * WIDE : (c + 1) * WIDE]
        main = jnp.dot(pick, part, preferred_element_type=F32)
        out_ref[:, first : first + WIDE] = main.astype(BF16)
        tail = spread_tail(part.astype(F32)).astype(BF16)
        last = jnp.dot(pick, tail, preferred_element_type=F32)
        out_ref[:, first + WIDE : first + CHUNK_HEADS * HD] = last.astype(BF16)


def call(kernel, name, out_shape, flops, moved, scratch=()):
    return pl.pallas_call(
        kernel,
        out_shape=out_shape,
        scratch_shapes=list(scratch),
        compiler_params=pltpu.CompilerParams(vmem_limit_bytes=VMEM_LIMIT),
        cost_estimate=pl.CostEstimate(flops=flops, bytes_accessed=moved, transcendentals=0),
        name=name,
    )


def exchange(rows, owners):
    shaped = rows.reshape(owners, TILE, rows.shape[1])
    return lax.all_to_all(shaped, "seq", split_axis=0, concat_axis=0, tiled=True).reshape(rows.shape)


def local(query_rows, key_rows, value_rows, owner_ids):
    owners = lax.axis_size("seq")
    spans = lax.axis_size("span")
    row_count = query_rows.shape[1]
    rows = owners * TILE
    own_rows = owners * SLOTS
    half = KVH * HD
    shape = jax.ShapeDtypeStruct

    send_kv = call(
        pack_kv_kernel, "pack_kv", shape((rows, 2 * half), BF16), rows * row_count * 4 * half, 4 * rows * half
    )(owner_ids, key_rows[0], value_rows[0])
    send_q = call(
        pack_q_kernel,
        "pack_q",
        shape((rows, CHUNKS * WIDE), BF16),
        4 * rows * row_count * HQ * HD,
        4 * rows * HQ * HD,
    )(owner_ids, query_rows[0])
    got_kv, send_q = lax.optimization_barrier((exchange(send_kv, owners), send_q))
    got_q = exchange(send_q, owners)
    own_kv, fold, unfold = call(
        compact_kernel,
        "compact",
        [
            shape((own_rows + TILE, 2 * half), BF16),
            shape((own_rows, rows), BF16),
            shape((rows, own_rows), BF16),
        ],
        2 * own_rows * rows * 2 * half,
        8 * rows * half,
    )(got_kv)
    all_kv = lax.all_gather(own_kv, "span", axis=0)
    most_keys = spans * own_rows
    key_blocks = -(-most_keys // KEY_BLOCK)
    done = call(
        attend_kernel,
        "attend",
        shape((rows, CHUNKS * WIDE), BF16),
        4 * own_rows * own_rows * spans * HD * HQ,
        8 * rows * HQ * HD,
        [
            pltpu.VMEM((rows, HQ * HD), BF16),
            pltpu.VMEM((own_rows, HQ * HD), BF16),
            pltpu.VMEM((key_blocks * KEY_BLOCK, half), BF16),
            pltpu.VMEM((key_blocks * KEY_BLOCK, half), BF16),
            pltpu.VMEM((key_blocks, half, KEY_BLOCK), BF16),
            pltpu.VMEM((key_blocks * KEY_BLOCK, HD), F32),
            pltpu.SMEM((spans,), jnp.int32),
        ],
    )(got_q, all_kv, fold, unfold)
    result = call(
        unpack_kernel,
        "unpack",
        shape((row_count, HQ * HD), BF16),
        4 * rows * row_count * HQ * HD,
        4 * rows * HQ * HD,
    )(owner_ids, exchange(done, owners))
    return result[None]


def solution(mesh):
    return jax.shard_map(
        local,
        mesh=mesh,
        in_specs=(
            P("span", "seq", None),
            P("span", "seq", None),
            P("span", "seq", None),
            P("span", "seq"),
        ),
        out_specs=P("span", "seq", None),
        check_vma=False,
    )
```

```python
import functools
import math

import jax
import jax.numpy as jnp
from jax import lax
from jax.experimental import pallas as pl
from jax.experimental.pallas import tpu as pltpu
from jax.sharding import PartitionSpec as P

HQ = 24
KVH = 4
HD = 128
GROUP = HQ // KVH
TILE = 8
SLOTS = 7
WIDE = SLOTS * HD
BACK = GROUP * HD
KEY_BLOCK = 256
QUERY_BLOCK = 128
ALIGN = 16
EMPTY = 2.0**100
F32 = jnp.float32
BF16 = jnp.bfloat16
VMEM_LIMIT = 48 << 20


def iota(shape, dim):
    return lax.broadcasted_iota(jnp.int32, shape, dim)


def row_ranks(owner_ref, axis):
    count = owner_ref.shape[1]
    along = jnp.broadcast_to(owner_ref[...].astype(F32), (count, count))
    down = along.T
    earlier = (along == down) & (iota((count, count), axis) < iota((count, count), 1 - axis))
    rank = jnp.sum(jnp.where(earlier, 1.0, 0.0), axis=axis, keepdims=True)
    owner = owner_ref[...] if axis == 0 else down[:, :1].astype(jnp.int32)
    return owner, rank.astype(jnp.int32)


def one_hot(condition):
    return jnp.where(condition, 1.0, 0.0).astype(BF16)


def pack_kernel(owner_ref, query_ref, key_ref, value_ref, out_ref):
    owner, rank = row_ranks(owner_ref, 0)
    count = owner.shape[1]
    rows = out_ref.shape[0] // KVH
    place = iota((rows, count), 0)
    chosen = jnp.where(place == owner * TILE + rank, 1.0, 0.0)
    filled = jnp.sum(chosen, axis=1, keepdims=True)
    slot = (iota((rows, 1), 0) & (TILE - 1)) < SLOTS
    mark = jnp.where(slot & (filled == 0.0), F32(EMPTY), F32(0.0))
    select = chosen.astype(BF16)
    spare = place == owner * TILE + SLOTS
    tails = [
        jnp.dot(one_hot(spare & (rank == k)), value_ref[...], preferred_element_type=F32) for k in range(SLOTS)
    ]
    for c in range(KVH):
        at = slice(c * rows, (c + 1) * rows)
        own = slice(c * HD, (c + 1) * HD)
        keys = jnp.dot(select, key_ref[:, own], preferred_element_type=F32)
        out_ref[at, :HD] = (keys + mark + tails[0][:, own]).astype(BF16)
        queries = jnp.dot(select, query_ref[:, c * BACK : (c + 1) * BACK], preferred_element_type=F32)
        rest = jnp.concatenate([tails[k][:, own] for k in range(1, SLOTS)], axis=1)
        out_ref[at, HD:] = (queries + rest).astype(BF16)


def spread_tail(spare_rows):
    tiles = spare_rows.shape[0]
    sub = iota((tiles, TILE, HD), 1)
    tail = jnp.zeros((tiles, TILE, HD), F32)
    for k in range(SLOTS):
        piece = jnp.broadcast_to(spare_rows[:, :, k * HD : (k + 1) * HD], (tiles, TILE, HD))
        tail = jnp.where(sub == k, piece, tail)
    return tail.reshape(tiles * TILE, HD)


def attend_kernel(
    got_ref, out_ref, x_ref, before_ref, k_ref, v_ref, turned_ref, bias_ref, query_ref, held_ref, sem
):
    spans = x_ref.shape[0]
    rows = x_ref.shape[1]
    blocks = query_ref.shape[0]
    lanes = GROUP * QUERY_BLOCK
    factor = F32(math.log2(math.e) / math.sqrt(HD))

    def arrival(t):
        source = got_ref.at[pl.ds(t * rows, rows), :]
        return pltpu.make_async_copy(source, x_ref.at[t, :, pl.ds(0, WIDE)], sem.at[t])

    for t in range(spans):
        arrival(t).start()
    before_ref[...] = one_hot(iota((rows, rows), 1) < iota((rows, rows), 0))
    k_ref[...] = jnp.zeros_like(k_ref)
    v_ref[...] = jnp.zeros_like(v_ref)
    bias_ref[...] = jnp.full(bias_ref.shape, -1e30, F32)
    offset = jnp.int32(0)
    for t in range(spans):
        arrival(t).wait()
        spare_rows = x_ref[t, :, :WIDE].astype(F32).reshape(rows // TILE, TILE, WIDE)[:, SLOTS:, :]
        x_ref[t, :, WIDE:] = spread_tail(spare_rows).astype(BF16)
        marks = x_ref[t, :, :HD].astype(F32)
        valid = (marks < F32(EMPTY / 2)) & ((iota((rows, HD), 0) & (TILE - 1)) < SLOTS)
        ahead = jnp.dot(before_ref[...], one_hot(valid), preferred_element_type=F32)
        down = jnp.where(valid, ahead, -1.0)
        along = down.T[:1].astype(jnp.int32)
        total = (jnp.max(down) + 1.0).astype(jnp.int32)
        count = (total + QUERY_BLOCK - 1) // QUERY_BLOCK

        def gather_block(i, _):
            fold = one_hot(iota((QUERY_BLOCK, rows), 0) + i * QUERY_BLOCK == along)
            dense = jnp.dot(fold, x_ref[t], preferred_element_type=F32)
            at = pl.ds(pl.multiple_of(offset + i * QUERY_BLOCK, ALIGN), QUERY_BLOCK)
            k_ref[at, :] = dense[:, :HD].astype(BF16)
            v_ref[at, :] = dense[:, WIDE:]
            inside = iota((QUERY_BLOCK, HD), 0) + i * QUERY_BLOCK < total
            bias_ref[at, :] = jnp.where(inside, F32(0.0), F32(-1e30))
            stack = jnp.concatenate([dense[:, (1 + h) * HD : (2 + h) * HD] for h in range(GROUP)], axis=0)
            query_ref[i] = stack.T.astype(BF16)
            return 0

        lax.fori_loop(0, count, gather_block, 0)
        end = offset + total

        def turn_block(b, _):
            at = pl.ds(pl.multiple_of(b * KEY_BLOCK, KEY_BLOCK), KEY_BLOCK)
            turned_ref[:, at] = v_ref[at, :].T.astype(BF16)
            return 0

        key_blocks = (end + KEY_BLOCK - 1) // KEY_BLOCK
        lax.fori_loop(offset // KEY_BLOCK, key_blocks, turn_block, 0)

        def attend_block(i, used):
            keys = used * KEY_BLOCK
            bias = jnp.concatenate([bias_ref[:keys, :]] * (lanes // HD), axis=1)
            scores = jnp.dot(k_ref[:keys, :], query_ref[i], preferred_element_type=F32) * factor + bias
            weights = jnp.exp2(scores - jnp.max(scores, axis=0, keepdims=True))
            total = jnp.sum(weights, axis=0, keepdims=True)
            accum = jnp.dot(turned_ref[:, :keys], weights.astype(BF16), preferred_element_type=F32)
            result = (accum / total).T.astype(BF16)
            at = pl.ds(pl.multiple_of(i * QUERY_BLOCK, QUERY_BLOCK), QUERY_BLOCK)
            for h in range(GROUP):
                held_ref[at, h * HD : (h + 1) * HD] = result[h * QUERY_BLOCK : (h + 1) * QUERY_BLOCK]

        def query_step(i, _):
            for used in range(1, turned_ref.shape[1] // KEY_BLOCK + 1):
                pl.when(key_blocks == used)(functools.partial(attend_block, i, used))
            return 0

        lax.fori_loop(0, count, query_step, 0)

        def clear_block(i, _):
            at = pl.ds(pl.multiple_of(i * QUERY_BLOCK, QUERY_BLOCK), QUERY_BLOCK)
            held_ref[at, :] = jnp.zeros((QUERY_BLOCK, BACK), BF16)
            return 0

        lax.fori_loop(count, blocks, clear_block, 0)
        slots = blocks * QUERY_BLOCK
        wide = jnp.concatenate([down] * (-(-slots // HD)), axis=1)[:, :slots]
        unfold = one_hot(wide == iota((rows, slots), 1).astype(F32))
        moved = jnp.dot(unfold, held_ref[...], preferred_element_type=F32)
        out_ref[t * rows : (t + 1) * rows, :] = moved.astype(BF16)
        offset = offset + (total + ALIGN - 1) // ALIGN * ALIGN


def unpack_kernel(owner_ref, got_ref, out_ref):
    owner, rank = row_ranks(owner_ref, 1)
    count = owner.shape[0]
    rows = got_ref.shape[0] // KVH
    pick = one_hot(iota((count, rows), 1) == owner * TILE + rank)
    for c in range(KVH):
        moved = jnp.dot(pick, got_ref[c * rows : (c + 1) * rows, :], preferred_element_type=F32)
        out_ref[:, c * BACK : (c + 1) * BACK] = moved.astype(BF16)


def call(kernel, name, out_shape, flops, moved, scratch=(), **specs):
    return pl.pallas_call(
        kernel,
        out_shape=out_shape,
        scratch_shapes=list(scratch),
        compiler_params=pltpu.CompilerParams(vmem_limit_bytes=VMEM_LIMIT),
        cost_estimate=pl.CostEstimate(flops=flops, bytes_accessed=moved, transcendentals=0),
        name=name,
        **specs,
    )


def exchange(rows):
    shaped = rows.reshape(rows.shape[0] // TILE, TILE, rows.shape[1])
    return lax.all_to_all(shaped, ("span", "seq"), split_axis=0, concat_axis=0, tiled=True).reshape(rows.shape)


def attend(got, owners, spans):
    rows = owners * TILE
    own_rows = owners * SLOTS
    key_blocks = -(-(spans * own_rows + QUERY_BLOCK) // KEY_BLOCK)
    key_rows = key_blocks * KEY_BLOCK
    return call(
        attend_kernel,
        "attend",
        jax.ShapeDtypeStruct((spans * rows, BACK), BF16),
        4 * own_rows * own_rows * spans * spans * HD * GROUP,
        4 * spans * rows * WIDE,
        [
            pltpu.VMEM((spans, rows, WIDE + HD), BF16),
            pltpu.VMEM((rows, rows), BF16),
            pltpu.VMEM((key_rows, HD), BF16),
            pltpu.VMEM((key_rows, HD), F32),
            pltpu.VMEM((HD, key_rows), BF16),
            pltpu.VMEM((key_rows, HD), F32),
            pltpu.VMEM((-(-own_rows // QUERY_BLOCK), HD, GROUP * QUERY_BLOCK), BF16),
            pltpu.VMEM((-(-own_rows // QUERY_BLOCK) * QUERY_BLOCK, BACK), BF16),
            pltpu.SemaphoreType.DMA((spans,)),
        ],
        in_specs=[pl.BlockSpec(memory_space=pl.ANY)],
    )(got)


def local(query_rows, key_rows, value_rows, owner_ids):
    owners = lax.axis_size("seq")
    spans = lax.axis_size("span")
    row_count = query_rows.shape[1]
    rows = owners * TILE
    shape = jax.ShapeDtypeStruct
    send = call(
        pack_kernel,
        "pack",
        shape((KVH * rows, WIDE), BF16),
        4 * rows * row_count * HQ * HD,
        8 * rows * WIDE,
    )(owner_ids, query_rows[0], key_rows[0], value_rows[0])
    done = attend(exchange(send), owners, spans)
    result = call(
        unpack_kernel,
        "unpack",
        shape((row_count, HQ * HD), BF16),
        2 * rows * row_count * HQ * HD,
        4 * rows * HQ * HD,
    )(owner_ids, exchange(done))
    return result[None]


def solution(mesh):
    return jax.shard_map(
        local,
        mesh=mesh,
        in_specs=(
            P("span", "seq", None),
            P("span", "seq", None),
            P("span", "seq", None),
            P("span", "seq"),
        ),
        out_specs=P("span", "seq", None),
        check_vma=False,
    )
```

```python
import functools
import math

import jax
import jax.numpy as jnp
from jax import lax
from jax.experimental import pallas as pl
from jax.experimental.pallas import tpu as pltpu
from jax.sharding import PartitionSpec as P

HQ = 24
KVH = 4
HD = 128
GROUP = HQ // KVH
TILE = 8
SLOTS = 7
WIDE = SLOTS * HD
BACK = GROUP * HD
KEY_BLOCK = 256
QUERY_BLOCK = 128
ALIGN = 16
EMPTY = 2.0**100
F32 = jnp.float32
BF16 = jnp.bfloat16
VMEM_LIMIT = 48 << 20
PACK_LIMIT = 58 << 20


def iota(shape, dim):
    return lax.broadcasted_iota(jnp.int32, shape, dim)


def row_ranks(owner_ref, axis):
    count = owner_ref.shape[1]
    along = jnp.broadcast_to(owner_ref[...].astype(F32), (count, count))
    down = along.T
    earlier = (along == down) & (iota((count, count), axis) < iota((count, count), 1 - axis))
    rank = jnp.sum(jnp.where(earlier, 1.0, 0.0), axis=axis, keepdims=True)
    owner = owner_ref[...] if axis == 0 else down[:, :1].astype(jnp.int32)
    return owner, rank.astype(jnp.int32)


def one_hot(condition):
    return jnp.where(condition, 1.0, 0.0).astype(BF16)


def pack_kernel(
    owner_ref, query_hbm, key_hbm, value_hbm, out_hbm, query_ref, key_ref, value_ref, out_ref, sem, out_sem
):
    pairs = ((value_hbm, value_ref), (key_hbm, key_ref), (query_hbm, query_ref))
    copies = [pltpu.make_async_copy(source, target, sem.at[i]) for i, (source, target) in enumerate(pairs)]
    for copy in copies:
        copy.start()
    owner, rank = row_ranks(owner_ref, 0)
    count = owner.shape[1]
    rows = out_ref.shape[1]
    place = iota((rows, count), 0)
    chosen = jnp.where(place == owner * TILE + rank, 1.0, 0.0)
    filled = jnp.sum(chosen, axis=1, keepdims=True)
    slot = (iota((rows, 1), 0) & (TILE - 1)) < SLOTS
    mark = jnp.where(slot & (filled == 0.0), F32(EMPTY), F32(0.0))
    select = chosen.astype(BF16)
    spare = place == owner * TILE + SLOTS
    copies[0].wait()
    tails = [
        jnp.dot(one_hot(spare & (rank == k)), value_ref[...], preferred_element_type=F32) for k in range(SLOTS)
    ]
    copies[1].wait()
    copies[2].wait()
    leaving = []
    for c in range(KVH):
        own = slice(c * HD, (c + 1) * HD)
        keys = jnp.dot(select, key_ref[:, own], preferred_element_type=F32)
        out_ref[c, :, :HD] = (keys + mark + tails[0][:, own]).astype(BF16)
        queries = jnp.dot(select, query_ref[:, c * BACK : (c + 1) * BACK], preferred_element_type=F32)
        rest = jnp.concatenate([tails[k][:, own] for k in range(1, SLOTS)], axis=1)
        out_ref[c, :, HD:] = (queries + rest).astype(BF16)
        leave = pltpu.make_async_copy(out_ref.at[c], out_hbm.at[pl.ds(c * rows, rows), :], out_sem.at[c])
        leave.start()
        leaving.append(leave)
    for leave in leaving:
        leave.wait()


def spread_tail(spare_rows):
    tiles = spare_rows.shape[0]
    sub = iota((tiles, TILE, HD), 1)
    tail = jnp.zeros((tiles, TILE, HD), F32)
    for k in range(SLOTS):
        piece = jnp.broadcast_to(spare_rows[:, :, k * HD : (k + 1) * HD], (tiles, TILE, HD))
        tail = jnp.where(sub == k, piece, tail)
    return tail.reshape(tiles * TILE, HD)


def attend_kernel(
    got_ref, out_ref, x_ref, before_ref, k_ref, v_ref, turned_ref, bias_ref, query_ref, held_ref, score_ref, sem
):
    spans = x_ref.shape[0]
    rows = x_ref.shape[1]
    blocks = query_ref.shape[0]
    lanes = GROUP * QUERY_BLOCK
    factor = F32(math.log2(math.e) / math.sqrt(HD))

    def arrival(t):
        source = got_ref.at[pl.ds(pl.multiple_of(t * rows, rows), rows), :]
        return pltpu.make_async_copy(source, x_ref.at[t, :, pl.ds(0, WIDE)], sem.at[t])

    for t in range(spans):
        arrival(t).start()
    before_ref[...] = one_hot(iota((rows, rows), 1) < iota((rows, rows), 0))
    k_ref[...] = jnp.zeros_like(k_ref)
    v_ref[...] = jnp.zeros_like(v_ref)
    bias_ref[...] = jnp.full(bias_ref.shape, -1e30, F32)

    def span_step(t, offset):
        arrival(t).wait()
        spare_rows = x_ref[t, :, :WIDE].astype(F32).reshape(rows // TILE, TILE, WIDE)[:, SLOTS:, :]
        x_ref[t, :, WIDE:] = spread_tail(spare_rows).astype(BF16)
        marks = x_ref[t, :, :HD].astype(F32)
        valid = (marks < F32(EMPTY / 2)) & ((iota((rows, HD), 0) & (TILE - 1)) < SLOTS)
        ahead = jnp.dot(before_ref[...], one_hot(valid), preferred_element_type=F32)
        down = jnp.where(valid, ahead, -1.0)
        along = down.T[:1].astype(jnp.int32)
        total = (jnp.max(down) + 1.0).astype(jnp.int32)
        count = (total + QUERY_BLOCK - 1) // QUERY_BLOCK

        def gather_block(i, _):
            fold = one_hot(iota((QUERY_BLOCK, rows), 0) + i * QUERY_BLOCK == along)
            dense = jnp.dot(fold, x_ref[t], preferred_element_type=F32)
            at = pl.ds(pl.multiple_of(offset + i * QUERY_BLOCK, ALIGN), QUERY_BLOCK)
            k_ref[at, :] = dense[:, :HD].astype(BF16)
            v_ref[at, :] = dense[:, WIDE:]
            inside = iota((QUERY_BLOCK, HD), 0) + i * QUERY_BLOCK < total
            bias_ref[at, :] = jnp.where(inside, F32(0.0), F32(-1e30))
            stack = jnp.concatenate([dense[:, (1 + h) * HD : (2 + h) * HD] for h in range(GROUP)], axis=0)
            query_ref[i] = stack.T.astype(BF16)
            return 0

        lax.fori_loop(0, count, gather_block, 0)
        end = offset + total

        def turn_block(b, _):
            at = pl.ds(pl.multiple_of(b * KEY_BLOCK, KEY_BLOCK), KEY_BLOCK)
            turned_ref[:, at] = v_ref[at, :].T.astype(BF16)
            return 0

        key_blocks = (end + KEY_BLOCK - 1) // KEY_BLOCK
        lax.fori_loop(offset // KEY_BLOCK, key_blocks, turn_block, 0)

        def attend_block(i, used):
            at = pl.ds(pl.multiple_of(i * QUERY_BLOCK, QUERY_BLOCK), QUERY_BLOCK)
            top = jnp.full((1, lanes), -1e30, F32)
            for b in range(used):
                part = slice(b * KEY_BLOCK, (b + 1) * KEY_BLOCK)
                bias = jnp.concatenate([bias_ref[part, :]] * (lanes // HD), axis=1)
                scores = jnp.dot(k_ref[part, :], query_ref[i], preferred_element_type=F32) * factor + bias
                score_ref[part, :] = scores
                top = jnp.maximum(top, jnp.max(scores, axis=0, keepdims=True))
            total = jnp.zeros((1, lanes), F32)
            accum = jnp.zeros((HD, lanes), F32)
            for b in range(used):
                part = slice(b * KEY_BLOCK, (b + 1) * KEY_BLOCK)
                weights = jnp.exp2(score_ref[part, :] - top)
                total = total + jnp.sum(weights, axis=0, keepdims=True)
                accum = accum + jnp.dot(turned_ref[:, part], weights.astype(BF16), preferred_element_type=F32)
            result = (accum / total).T.astype(BF16)
            for h in range(GROUP):
                held_ref[at, h * HD : (h + 1) * HD] = result[h * QUERY_BLOCK : (h + 1) * QUERY_BLOCK]

        def query_step(i, _):
            for used in range(1, turned_ref.shape[1] // KEY_BLOCK + 1):
                pl.when(key_blocks == used)(functools.partial(attend_block, i, used))
            return 0

        lax.fori_loop(0, count, query_step, 0)

        def clear_block(i, _):
            at = pl.ds(pl.multiple_of(i * QUERY_BLOCK, QUERY_BLOCK), QUERY_BLOCK)
            held_ref[at, :] = jnp.zeros((QUERY_BLOCK, BACK), BF16)
            return 0

        lax.fori_loop(count, blocks, clear_block, 0)
        slots = blocks * QUERY_BLOCK
        wide = jnp.concatenate([down] * (-(-slots // HD)), axis=1)[:, :slots]
        unfold = one_hot(wide == iota((rows, slots), 1).astype(F32))
        moved = jnp.dot(unfold, held_ref[...], preferred_element_type=F32)
        out_ref[pl.ds(pl.multiple_of(t * rows, rows), rows), :] = moved.astype(BF16)
        return offset + (total + ALIGN - 1) // ALIGN * ALIGN

    lax.fori_loop(0, spans, span_step, jnp.int32(0))


def unpack_kernel(owner_ref, got_ref, out_ref):
    owner, rank = row_ranks(owner_ref, 1)
    count = owner.shape[0]
    rows = got_ref.shape[0] // KVH
    pick = one_hot(iota((count, rows), 1) == owner * TILE + rank)
    for c in range(KVH):
        moved = jnp.dot(pick, got_ref[c * rows : (c + 1) * rows, :], preferred_element_type=F32)
        out_ref[:, c * BACK : (c + 1) * BACK] = moved.astype(BF16)


def call(kernel, name, out_shape, flops, moved, scratch=(), limit=VMEM_LIMIT, **specs):
    return pl.pallas_call(
        kernel,
        out_shape=out_shape,
        scratch_shapes=list(scratch),
        compiler_params=pltpu.CompilerParams(vmem_limit_bytes=limit),
        cost_estimate=pl.CostEstimate(flops=flops, bytes_accessed=moved, transcendentals=0),
        name=name,
        **specs,
    )


def exchange(rows):
    shaped = rows.reshape(rows.shape[0] // TILE, TILE, rows.shape[1])
    return lax.all_to_all(shaped, ("span", "seq"), split_axis=0, concat_axis=0, tiled=True).reshape(rows.shape)


def attend(got, owners, spans):
    rows = owners * TILE
    own_rows = owners * SLOTS
    key_blocks = -(-(spans * own_rows + QUERY_BLOCK) // KEY_BLOCK)
    key_rows = key_blocks * KEY_BLOCK
    return call(
        attend_kernel,
        "attend",
        jax.ShapeDtypeStruct((spans * rows, BACK), BF16),
        4 * own_rows * own_rows * spans * spans * HD * GROUP,
        4 * spans * rows * WIDE,
        [
            pltpu.VMEM((spans, rows, WIDE + HD), BF16),
            pltpu.VMEM((rows, rows), BF16),
            pltpu.VMEM((key_rows, HD), BF16),
            pltpu.VMEM((key_rows, HD), F32),
            pltpu.VMEM((HD, key_rows), BF16),
            pltpu.VMEM((key_rows, HD), F32),
            pltpu.VMEM((-(-own_rows // QUERY_BLOCK), HD, GROUP * QUERY_BLOCK), BF16),
            pltpu.VMEM((-(-own_rows // QUERY_BLOCK) * QUERY_BLOCK, BACK), BF16),
            pltpu.VMEM((key_rows, GROUP * QUERY_BLOCK), F32),
            pltpu.SemaphoreType.DMA((spans,)),
        ],
        in_specs=[pl.BlockSpec(memory_space=pl.ANY)],
    )(got)


def local(query_rows, key_rows, value_rows, owner_ids):
    owners = lax.axis_size("seq")
    spans = lax.axis_size("span")
    row_count = query_rows.shape[1]
    rows = owners * TILE
    shape = jax.ShapeDtypeStruct
    send = call(
        pack_kernel,
        "pack",
        shape((KVH * rows, WIDE), BF16),
        4 * rows * row_count * HQ * HD,
        8 * rows * WIDE,
        [
            pltpu.VMEM((row_count, HQ * HD), BF16),
            pltpu.VMEM((row_count, KVH * HD), BF16),
            pltpu.VMEM((row_count, KVH * HD), BF16),
            pltpu.VMEM((KVH, rows, WIDE), BF16),
            pltpu.SemaphoreType.DMA((3,)),
            pltpu.SemaphoreType.DMA((KVH,)),
        ],
        limit=PACK_LIMIT,
        in_specs=[pl.BlockSpec(memory_space=pltpu.VMEM)] + [pl.BlockSpec(memory_space=pl.ANY)] * 3,
        out_specs=pl.BlockSpec(memory_space=pl.ANY),
    )(owner_ids, query_rows[0], key_rows[0], value_rows[0])
    done = attend(exchange(send), owners, spans)
    result = call(
        unpack_kernel,
        "unpack",
        shape((row_count, HQ * HD), BF16),
        2 * rows * row_count * HQ * HD,
        4 * rows * HQ * HD,
    )(owner_ids, exchange(done))
    return result[None]


def solution(mesh):
    return jax.shard_map(
        local,
        mesh=mesh,
        in_specs=(
            P("span", "seq", None),
            P("span", "seq", None),
            P("span", "seq", None),
            P("span", "seq"),
        ),
        out_specs=P("span", "seq", None),
        check_vma=False,
    )
```

```python
import functools
import math

import jax
import jax.numpy as jnp
from jax import lax
from jax.experimental import pallas as pl
from jax.experimental.pallas import tpu as pltpu
from jax.sharding import PartitionSpec as P

HQ = 24
KVH = 4
HD = 128
GROUP = HQ // KVH
TILE = 8
SLOTS = 7
WIDE = SLOTS * HD
BACK = GROUP * HD
KEY_BLOCK = 256
QUERY_BLOCK = 128
HALF_BLOCK = QUERY_BLOCK // 2
ALIGN = 16
EMPTY = 2.0**100
F32 = jnp.float32
BF16 = jnp.bfloat16
VMEM_LIMIT = 48 << 20
PACK_LIMIT = 58 << 20


def iota(shape, dim):
    return lax.broadcasted_iota(jnp.int32, shape, dim)


def row_ranks(owner_ref, axis):
    count = owner_ref.shape[1]
    along = jnp.broadcast_to(owner_ref[...].astype(F32), (count, count))
    down = along.T
    earlier = (along == down) & (iota((count, count), axis) < iota((count, count), 1 - axis))
    rank = jnp.sum(jnp.where(earlier, 1.0, 0.0), axis=axis, keepdims=True)
    owner = owner_ref[...] if axis == 0 else down[:, :1].astype(jnp.int32)
    return owner, rank.astype(jnp.int32)


def one_hot(condition):
    return jnp.where(condition, 1.0, 0.0).astype(BF16)


def pack_kernel(
    owner_ref, query_hbm, key_hbm, value_hbm, out_hbm, query_ref, key_ref, value_ref, out_ref, sem, out_sem
):
    pairs = ((value_hbm, value_ref), (key_hbm, key_ref), (query_hbm, query_ref))
    copies = [pltpu.make_async_copy(source, target, sem.at[i]) for i, (source, target) in enumerate(pairs)]
    for copy in copies:
        copy.start()
    owner, rank = row_ranks(owner_ref, 0)
    count = owner.shape[1]
    rows = out_ref.shape[1]
    place = iota((rows, count), 0)
    chosen = jnp.where(place == owner * TILE + rank, 1.0, 0.0)
    filled = jnp.sum(chosen, axis=1, keepdims=True)
    slot = (iota((rows, 1), 0) & (TILE - 1)) < SLOTS
    mark = jnp.where(slot & (filled == 0.0), F32(EMPTY), F32(0.0))
    select = chosen.astype(BF16)
    spare = place == owner * TILE + SLOTS
    copies[0].wait()
    tails = [
        jnp.dot(one_hot(spare & (rank == k)), value_ref[...], preferred_element_type=F32) for k in range(SLOTS)
    ]
    copies[1].wait()
    copies[2].wait()
    leaving = []
    for c in range(KVH):
        own = slice(c * HD, (c + 1) * HD)
        keys = jnp.dot(select, key_ref[:, own], preferred_element_type=F32)
        out_ref[c, :, :HD] = (keys + mark + tails[0][:, own]).astype(BF16)
        queries = jnp.dot(select, query_ref[:, c * BACK : (c + 1) * BACK], preferred_element_type=F32)
        rest = jnp.concatenate([tails[k][:, own] for k in range(1, SLOTS)], axis=1)
        out_ref[c, :, HD:] = (queries + rest).astype(BF16)
        leave = pltpu.make_async_copy(out_ref.at[c], out_hbm.at[pl.ds(c * rows, rows), :], out_sem.at[c])
        leave.start()
        leaving.append(leave)
    for leave in leaving:
        leave.wait()


def spread_tail(spare_rows):
    tiles = spare_rows.shape[0]
    sub = iota((tiles, TILE, HD), 1)
    tail = jnp.zeros((tiles, TILE, HD), F32)
    for k in range(SLOTS):
        piece = jnp.broadcast_to(spare_rows[:, :, k * HD : (k + 1) * HD], (tiles, TILE, HD))
        tail = jnp.where(sub == k, piece, tail)
    return tail.reshape(tiles * TILE, HD)


def attend_kernel(
    got_ref, out_ref, x_ref, before_ref, k_ref, v_ref, turned_ref, bias_ref, query_ref, held_ref, score_ref, sem
):
    spans = x_ref.shape[0]
    rows = x_ref.shape[1]
    blocks = query_ref.shape[0]
    factor = F32(math.log2(math.e) / math.sqrt(HD))

    def arrival(t):
        source = got_ref.at[pl.ds(pl.multiple_of(t * rows, rows), rows), :]
        return pltpu.make_async_copy(source, x_ref.at[t, :, pl.ds(0, WIDE)], sem.at[t])

    for t in range(spans):
        arrival(t).start()
    before_ref[...] = one_hot(iota((rows, rows), 1) < iota((rows, rows), 0))
    k_ref[...] = jnp.zeros_like(k_ref)
    v_ref[...] = jnp.zeros_like(v_ref)
    bias_ref[...] = jnp.full(bias_ref.shape, -1e30, F32)

    def span_step(t, offset):
        arrival(t).wait()
        spare_rows = x_ref[t, :, :WIDE].astype(F32).reshape(rows // TILE, TILE, WIDE)[:, SLOTS:, :]
        x_ref[t, :, WIDE:] = spread_tail(spare_rows).astype(BF16)
        marks = x_ref[t, :, :HD].astype(F32)
        valid = (marks < F32(EMPTY / 2)) & ((iota((rows, HD), 0) & (TILE - 1)) < SLOTS)
        ahead = jnp.dot(before_ref[...], one_hot(valid), preferred_element_type=F32)
        down = jnp.where(valid, ahead, -1.0)
        along = down.T[:1].astype(jnp.int32)
        total = (jnp.max(down) + 1.0).astype(jnp.int32)
        halves = (total + HALF_BLOCK - 1) // HALF_BLOCK
        count = halves // 2
        odd = halves % 2 == 1

        def gather_block(size, i):
            fold = one_hot(iota((size, rows), 0) + i * QUERY_BLOCK == along)
            dense = jnp.dot(fold, x_ref[t], preferred_element_type=F32)
            at = pl.ds(pl.multiple_of(offset + i * QUERY_BLOCK, ALIGN), size)
            k_ref[at, :] = dense[:, :HD].astype(BF16)
            v_ref[at, :] = dense[:, WIDE:]
            inside = iota((size, HD), 0) + i * QUERY_BLOCK < total
            bias_ref[at, :] = jnp.where(inside, F32(0.0), F32(-1e30))
            stack = jnp.concatenate([dense[:, (1 + h) * HD : (2 + h) * HD] for h in range(GROUP)], axis=0)
            query_ref[i, :, : GROUP * size] = stack.T.astype(BF16)

        def whole_block(i, _):
            gather_block(QUERY_BLOCK, i)
            return 0

        lax.fori_loop(0, count, whole_block, 0)
        pl.when(odd)(functools.partial(gather_block, HALF_BLOCK, count))
        end = offset + total

        def turn_block(b, _):
            at = pl.ds(pl.multiple_of(b * KEY_BLOCK, KEY_BLOCK), KEY_BLOCK)
            turned_ref[:, at] = v_ref[at, :].T.astype(BF16)
            return 0

        key_blocks = (end + KEY_BLOCK - 1) // KEY_BLOCK
        lax.fori_loop(offset // KEY_BLOCK, key_blocks, turn_block, 0)

        def attend_block(size, i, used):
            lanes = GROUP * size
            query = query_ref[i, :, :lanes]
            at = pl.ds(pl.multiple_of(i * QUERY_BLOCK, HALF_BLOCK), size)
            top = jnp.full((1, lanes), -1e30, F32)
            for b in range(used):
                part = slice(b * KEY_BLOCK, (b + 1) * KEY_BLOCK)
                bias = jnp.concatenate([bias_ref[part, :]] * (lanes // HD), axis=1)
                scores = jnp.dot(k_ref[part, :], query, preferred_element_type=F32) * factor + bias
                score_ref[part, :lanes] = scores
                top = jnp.maximum(top, jnp.max(scores, axis=0, keepdims=True))
            total = jnp.zeros((1, lanes), F32)
            accum = jnp.zeros((HD, lanes), F32)
            for b in range(used):
                part = slice(b * KEY_BLOCK, (b + 1) * KEY_BLOCK)
                weights = jnp.exp2(score_ref[part, :lanes] - top)
                total = total + jnp.sum(weights, axis=0, keepdims=True)
                accum = accum + jnp.dot(turned_ref[:, part], weights.astype(BF16), preferred_element_type=F32)
            result = (accum / total).T.astype(BF16)
            for h in range(GROUP):
                held_ref[at, h * HD : (h + 1) * HD] = result[h * size : (h + 1) * size]

        def by_keys(size, i):
            for used in range(1, turned_ref.shape[1] // KEY_BLOCK + 1):
                pl.when(key_blocks == used)(functools.partial(attend_block, size, i, used))

        def query_step(i, _):
            by_keys(QUERY_BLOCK, i)
            return 0

        lax.fori_loop(0, count, query_step, 0)
        pl.when(odd)(functools.partial(by_keys, HALF_BLOCK, count))

        def clear_block(i, _):
            at = pl.ds(pl.multiple_of(i * HALF_BLOCK, HALF_BLOCK), HALF_BLOCK)
            held_ref[at, :] = jnp.zeros((HALF_BLOCK, BACK), BF16)
            return 0

        lax.fori_loop(halves, blocks * QUERY_BLOCK // HALF_BLOCK, clear_block, 0)
        slots = blocks * QUERY_BLOCK
        wide = jnp.concatenate([down] * (-(-slots // HD)), axis=1)[:, :slots]
        unfold = one_hot(wide == iota((rows, slots), 1).astype(F32))
        moved = jnp.dot(unfold, held_ref[...], preferred_element_type=F32)
        out_ref[pl.ds(pl.multiple_of(t * rows, rows), rows), :] = moved.astype(BF16)
        return offset + (total + ALIGN - 1) // ALIGN * ALIGN

    lax.fori_loop(0, spans, span_step, jnp.int32(0))


def unpack_kernel(owner_ref, got_ref, out_ref):
    owner, rank = row_ranks(owner_ref, 1)
    count = owner.shape[0]
    rows = got_ref.shape[0] // KVH
    pick = one_hot(iota((count, rows), 1) == owner * TILE + rank)
    for c in range(KVH):
        moved = jnp.dot(pick, got_ref[c * rows : (c + 1) * rows, :], preferred_element_type=F32)
        out_ref[:, c * BACK : (c + 1) * BACK] = moved.astype(BF16)


def call(kernel, name, out_shape, flops, moved, scratch=(), limit=VMEM_LIMIT, **specs):
    return pl.pallas_call(
        kernel,
        out_shape=out_shape,
        scratch_shapes=list(scratch),
        compiler_params=pltpu.CompilerParams(vmem_limit_bytes=limit),
        cost_estimate=pl.CostEstimate(flops=flops, bytes_accessed=moved, transcendentals=0),
        name=name,
        **specs,
    )


def exchange(rows):
    shaped = rows.reshape(rows.shape[0] // TILE, TILE, rows.shape[1])
    return lax.all_to_all(shaped, ("span", "seq"), split_axis=0, concat_axis=0, tiled=True).reshape(rows.shape)


def attend(got, owners, spans):
    rows = owners * TILE
    own_rows = owners * SLOTS
    key_blocks = -(-(spans * own_rows + QUERY_BLOCK) // KEY_BLOCK)
    key_rows = key_blocks * KEY_BLOCK
    return call(
        attend_kernel,
        "attend",
        jax.ShapeDtypeStruct((spans * rows, BACK), BF16),
        4 * own_rows * own_rows * spans * spans * HD * GROUP,
        4 * spans * rows * WIDE,
        [
            pltpu.VMEM((spans, rows, WIDE + HD), BF16),
            pltpu.VMEM((rows, rows), BF16),
            pltpu.VMEM((key_rows, HD), BF16),
            pltpu.VMEM((key_rows, HD), F32),
            pltpu.VMEM((HD, key_rows), BF16),
            pltpu.VMEM((key_rows, HD), F32),
            pltpu.VMEM((-(-own_rows // QUERY_BLOCK), HD, GROUP * QUERY_BLOCK), BF16),
            pltpu.VMEM((-(-own_rows // QUERY_BLOCK) * QUERY_BLOCK, BACK), BF16),
            pltpu.VMEM((key_rows, GROUP * QUERY_BLOCK), F32),
            pltpu.SemaphoreType.DMA((spans,)),
        ],
        in_specs=[pl.BlockSpec(memory_space=pl.ANY)],
    )(got)


def local(query_rows, key_rows, value_rows, owner_ids):
    owners = lax.axis_size("seq")
    spans = lax.axis_size("span")
    row_count = query_rows.shape[1]
    rows = owners * TILE
    shape = jax.ShapeDtypeStruct
    send = call(
        pack_kernel,
        "pack",
        shape((KVH * rows, WIDE), BF16),
        4 * rows * row_count * HQ * HD,
        8 * rows * WIDE,
        [
            pltpu.VMEM((row_count, HQ * HD), BF16),
            pltpu.VMEM((row_count, KVH * HD), BF16),
            pltpu.VMEM((row_count, KVH * HD), BF16),
            pltpu.VMEM((KVH, rows, WIDE), BF16),
            pltpu.SemaphoreType.DMA((3,)),
            pltpu.SemaphoreType.DMA((KVH,)),
        ],
        limit=PACK_LIMIT,
        in_specs=[pl.BlockSpec(memory_space=pltpu.VMEM)] + [pl.BlockSpec(memory_space=pl.ANY)] * 3,
        out_specs=pl.BlockSpec(memory_space=pl.ANY),
    )(owner_ids, query_rows[0], key_rows[0], value_rows[0])
    done = attend(exchange(send), owners, spans)
    result = call(
        unpack_kernel,
        "unpack",
        shape((row_count, HQ * HD), BF16),
        2 * rows * row_count * HQ * HD,
        4 * rows * HQ * HD,
    )(owner_ids, exchange(done))
    return result[None]


def solution(mesh):
    return jax.shard_map(
        local,
        mesh=mesh,
        in_specs=(
            P("span", "seq", None),
            P("span", "seq", None),
            P("span", "seq", None),
            P("span", "seq"),
        ),
        out_specs=P("span", "seq", None),
        check_vma=False,
    )
```

```python
import functools
import math

import jax
import jax.numpy as jnp
from jax import lax
from jax.experimental import pallas as pl
from jax.experimental.pallas import tpu as pltpu
from jax.sharding import PartitionSpec as P

HQ = 24
KVH = 4
HD = 128
GROUP = HQ // KVH
TILE = 8
SLOTS = 7
WIDE = SLOTS * HD
BACK = GROUP * HD
FOUR = 4
LATE = SLOTS - FOUR
SIDE = (GROUP - 1) * HD
RETURNED = BACK + SIDE
KEY_BLOCK = 256
QUERY_BLOCK = 128
HALF_BLOCK = QUERY_BLOCK // 2
ALIGN = 16
EMPTY = 2.0**100
F32 = jnp.float32
BF16 = jnp.bfloat16
VMEM_LIMIT = 48 << 20
PACK_LIMIT = 58 << 20


def iota(shape, dim):
    return lax.broadcasted_iota(jnp.int32, shape, dim)


def row_ranks(owner_ref, axis):
    count = owner_ref.shape[1]
    along = jnp.broadcast_to(owner_ref[...].astype(F32), (count, count))
    down = along.T
    earlier = (along == down) & (iota((count, count), axis) < iota((count, count), 1 - axis))
    rank = jnp.sum(jnp.where(earlier, 1.0, 0.0), axis=axis, keepdims=True)
    owner = owner_ref[...] if axis == 0 else down[:, :1].astype(jnp.int32)
    return owner, rank.astype(jnp.int32)


def one_hot(condition):
    return jnp.where(condition, 1.0, 0.0).astype(BF16)


def pack_kernel(
    owner_ref, query_hbm, key_hbm, value_hbm, out_hbm, query_ref, key_ref, value_ref, out_ref, sem, out_sem
):
    pairs = ((value_hbm, value_ref), (key_hbm, key_ref), (query_hbm, query_ref))
    copies = [pltpu.make_async_copy(source, target, sem.at[i]) for i, (source, target) in enumerate(pairs)]
    for copy in copies:
        copy.start()
    owner, rank = row_ranks(owner_ref, 0)
    count = owner.shape[1]
    rows = out_ref.shape[1]
    place = iota((rows, count), 0)
    chosen = jnp.where(place == owner * TILE + rank, 1.0, 0.0)
    filled = jnp.sum(chosen, axis=1, keepdims=True)
    slot = (iota((rows, 1), 0) & (TILE - 1)) < SLOTS
    mark = jnp.where(slot & (filled == 0.0), F32(EMPTY), F32(0.0))
    select = chosen.astype(BF16)
    spare = place == owner * TILE + SLOTS
    copies[0].wait()
    tails = [
        jnp.dot(one_hot(spare & (rank == k)), value_ref[...], preferred_element_type=F32) for k in range(SLOTS)
    ]
    copies[1].wait()
    copies[2].wait()
    leaving = []
    for c in range(KVH):
        own = slice(c * HD, (c + 1) * HD)
        keys = jnp.dot(select, key_ref[:, own], preferred_element_type=F32)
        out_ref[c, :, :HD] = (keys + mark + tails[0][:, own]).astype(BF16)
        queries = jnp.dot(select, query_ref[:, c * BACK : (c + 1) * BACK], preferred_element_type=F32)
        rest = jnp.concatenate([tails[k][:, own] for k in range(1, SLOTS)], axis=1)
        out_ref[c, :, HD:] = (queries + rest).astype(BF16)
        leave = pltpu.make_async_copy(out_ref.at[c], out_hbm.at[pl.ds(c * rows, rows), :], out_sem.at[c])
        leave.start()
        leaving.append(leave)
    for leave in leaving:
        leave.wait()


def spread_tail(spare_rows):
    tiles = spare_rows.shape[0]
    sub = iota((tiles, TILE, HD), 1)
    tail = jnp.zeros((tiles, TILE, HD), F32)
    for k in range(SLOTS):
        piece = jnp.broadcast_to(spare_rows[:, :, k * HD : (k + 1) * HD], (tiles, TILE, HD))
        tail = jnp.where(sub == k, piece, tail)
    return tail.reshape(tiles * TILE, HD)


def returned_places(flags, first):
    rows = flags.shape[0]
    shape = (rows // TILE * FOUR, rows)
    line = iota(shape, 0)
    row = (line // FOUR) * TILE + (line & (FOUR - 1)) + first
    ahead = jnp.dot(one_hot(iota(shape, 1) < row), flags, preferred_element_type=F32)
    held = jnp.dot(one_hot(iota(shape, 1) == row), flags, preferred_element_type=F32)
    return jnp.where(held > 0.5, ahead, -1.0)


def picks(place, slots):
    wide = jnp.concatenate([place] * (slots // HD), axis=1)
    return one_hot(wide == iota(wide.shape, 1).astype(F32))


def attend_kernel(
    got_ref, out_ref, x_ref, before_ref, k_ref, v_ref, turned_ref, bias_ref, query_ref, held_ref, score_ref, sem
):
    spans = x_ref.shape[0]
    rows = x_ref.shape[1]
    blocks = query_ref.shape[0]
    factor = F32(math.log2(math.e) / math.sqrt(HD))

    def arrival(t):
        source = got_ref.at[pl.ds(pl.multiple_of(t * rows, rows), rows), :]
        return pltpu.make_async_copy(source, x_ref.at[t, :, pl.ds(0, WIDE)], sem.at[t])

    for t in range(spans):
        arrival(t).start()
    before_ref[...] = one_hot(iota((rows, rows), 1) < iota((rows, rows), 0))
    k_ref[...] = jnp.zeros_like(k_ref)
    v_ref[...] = jnp.zeros_like(v_ref)
    bias_ref[...] = jnp.full(bias_ref.shape, -1e30, F32)

    def span_step(t, offset):
        arrival(t).wait()
        spare_rows = x_ref[t, :, :WIDE].astype(F32).reshape(rows // TILE, TILE, WIDE)[:, SLOTS:, :]
        x_ref[t, :, WIDE:] = spread_tail(spare_rows).astype(BF16)
        marks = x_ref[t, :, :HD].astype(F32)
        valid = (marks < F32(EMPTY / 2)) & ((iota((rows, HD), 0) & (TILE - 1)) < SLOTS)
        ahead = jnp.dot(before_ref[...], one_hot(valid), preferred_element_type=F32)
        down = jnp.where(valid, ahead, -1.0)
        along = down.T[:1].astype(jnp.int32)
        total = (jnp.max(down) + 1.0).astype(jnp.int32)
        halves = (total + HALF_BLOCK - 1) // HALF_BLOCK
        count = halves // 2
        odd = halves % 2 == 1

        def gather_block(size, i):
            fold = one_hot(iota((size, rows), 0) + i * QUERY_BLOCK == along)
            dense = jnp.dot(fold, x_ref[t], preferred_element_type=F32)
            at = pl.ds(pl.multiple_of(offset + i * QUERY_BLOCK, ALIGN), size)
            k_ref[at, :] = dense[:, :HD].astype(BF16)
            v_ref[at, :] = dense[:, WIDE:]
            inside = iota((size, HD), 0) + i * QUERY_BLOCK < total
            bias_ref[at, :] = jnp.where(inside, F32(0.0), F32(-1e30))
            stack = jnp.concatenate([dense[:, (1 + h) * HD : (2 + h) * HD] for h in range(GROUP)], axis=0)
            query_ref[i, :, : GROUP * size] = stack.T.astype(BF16)

        def whole_block(i, _):
            gather_block(QUERY_BLOCK, i)
            return 0

        lax.fori_loop(0, count, whole_block, 0)
        pl.when(odd)(functools.partial(gather_block, HALF_BLOCK, count))
        end = offset + total

        def turn_block(b, _):
            at = pl.ds(pl.multiple_of(b * KEY_BLOCK, KEY_BLOCK), KEY_BLOCK)
            turned_ref[:, at] = v_ref[at, :].T.astype(BF16)
            return 0

        key_blocks = (end + KEY_BLOCK - 1) // KEY_BLOCK
        lax.fori_loop(offset // KEY_BLOCK, key_blocks, turn_block, 0)

        def attend_block(size, i, used):
            lanes = GROUP * size
            query = query_ref[i, :, :lanes]
            at = pl.ds(pl.multiple_of(i * QUERY_BLOCK, HALF_BLOCK), size)
            top = jnp.full((1, lanes), -1e30, F32)
            for b in range(used):
                part = slice(b * KEY_BLOCK, (b + 1) * KEY_BLOCK)
                bias = jnp.concatenate([bias_ref[part, :]] * (lanes // HD), axis=1)
                scores = jnp.dot(k_ref[part, :], query, preferred_element_type=F32) * factor + bias
                score_ref[part, :lanes] = scores
                top = jnp.maximum(top, jnp.max(scores, axis=0, keepdims=True))
            total = jnp.zeros((1, lanes), F32)
            accum = jnp.zeros((HD, lanes), F32)
            for b in range(used):
                part = slice(b * KEY_BLOCK, (b + 1) * KEY_BLOCK)
                weights = jnp.exp2(score_ref[part, :lanes] - top)
                total = total + jnp.sum(weights, axis=0, keepdims=True)
                accum = accum + jnp.dot(turned_ref[:, part], weights.astype(BF16), preferred_element_type=F32)
            result = (accum / total).T.astype(BF16)
            for h in range(GROUP):
                held_ref[at, h * HD : (h + 1) * HD] = result[h * size : (h + 1) * size]

        def by_keys(size, i):
            for used in range(1, turned_ref.shape[1] // KEY_BLOCK + 1):
                pl.when(key_blocks == used)(functools.partial(attend_block, size, i, used))

        def query_step(i, _):
            by_keys(QUERY_BLOCK, i)
            return 0

        lax.fori_loop(0, count, query_step, 0)
        pl.when(odd)(functools.partial(by_keys, HALF_BLOCK, count))

        def clear_block(i, _):
            at = pl.ds(pl.multiple_of(i * HALF_BLOCK, HALF_BLOCK), HALF_BLOCK)
            held_ref[at, :] = jnp.zeros((HALF_BLOCK, BACK), BF16)
            return 0

        lax.fori_loop(halves, blocks * QUERY_BLOCK // HALF_BLOCK, clear_block, 0)
        slots = blocks * QUERY_BLOCK
        flags = one_hot(valid)
        early = returned_places(flags, 0)
        late = returned_places(flags, FOUR)
        last = (iota((early.shape[0], HD), 0) & (FOUR - 1)) == FOUR - 1
        at = pl.ds(pl.multiple_of(t * (rows // TILE), rows // TILE), rows // TILE)
        moved = jnp.dot(picks(early, slots), held_ref[...], preferred_element_type=F32)
        out_ref[at, :, :BACK] = moved.astype(BF16).reshape(rows // TILE, FOUR, BACK)
        moved = jnp.dot(picks(late, slots), held_ref[:, :SIDE], preferred_element_type=F32)
        for j in range(GROUP - 1):
            piece = moved[:, j * HD : (j + 1) * HD]
            if j < LATE:
                place = jnp.where(last, pltpu.roll(late, FOUR - 1 - j, 0), -1.0)
                piece = piece + jnp.dot(picks(place, slots), held_ref[:, SIDE:], preferred_element_type=F32)
            lane = BACK + j * HD
            out_ref[at, :, lane : lane + HD] = piece.astype(BF16).reshape(rows // TILE, FOUR, HD)
        return offset + (total + ALIGN - 1) // ALIGN * ALIGN

    lax.fori_loop(0, spans, span_step, jnp.int32(0))


def unpack_kernel(owner_ref, got_ref, out_ref):
    owner, rank = row_ranks(owner_ref, 1)
    count = owner.shape[0]
    owners = got_ref.shape[0] // KVH
    lines = owners * FOUR
    line = iota((count, lines), 1)
    early = one_hot((line == owner * FOUR + rank) & (rank < FOUR))
    late = one_hot((line == owner * FOUR + rank - FOUR) & (rank >= FOUR))
    aside = line == owner * FOUR + FOUR - 1
    for c in range(KVH):
        part = got_ref[c * owners : (c + 1) * owners].reshape(lines, RETURNED)
        moved = jnp.dot(early, part[:, :BACK], preferred_element_type=F32)
        more = jnp.dot(late, part[:, BACK:], preferred_element_type=F32)
        out_ref[:, c * BACK : c * BACK + SIDE] = (moved[:, :SIDE] + more).astype(BF16)
        sixth = moved[:, SIDE:]
        for s in range(LATE):
            lane = BACK + s * HD
            chosen = one_hot(aside & (rank == FOUR + s))
            sixth = sixth + jnp.dot(chosen, part[:, lane : lane + HD], preferred_element_type=F32)
        out_ref[:, c * BACK + SIDE : (c + 1) * BACK] = sixth.astype(BF16)


def call(kernel, name, out_shape, flops, moved, scratch=(), limit=VMEM_LIMIT, **specs):
    return pl.pallas_call(
        kernel,
        out_shape=out_shape,
        scratch_shapes=list(scratch),
        compiler_params=pltpu.CompilerParams(vmem_limit_bytes=limit),
        cost_estimate=pl.CostEstimate(flops=flops, bytes_accessed=moved, transcendentals=0),
        name=name,
        **specs,
    )


def exchange(chunks):
    return lax.all_to_all(chunks, ("span", "seq"), split_axis=0, concat_axis=0, tiled=True)


def attend(got, owners, spans):
    rows = owners * TILE
    own_rows = owners * SLOTS
    key_blocks = -(-(spans * own_rows + QUERY_BLOCK) // KEY_BLOCK)
    key_rows = key_blocks * KEY_BLOCK
    return call(
        attend_kernel,
        "attend",
        jax.ShapeDtypeStruct((spans * owners, FOUR, RETURNED), BF16),
        4 * own_rows * own_rows * spans * spans * HD * GROUP,
        4 * spans * rows * WIDE,
        [
            pltpu.VMEM((spans, rows, WIDE + HD), BF16),
            pltpu.VMEM((rows, rows), BF16),
            pltpu.VMEM((key_rows, HD), BF16),
            pltpu.VMEM((key_rows, HD), F32),
            pltpu.VMEM((HD, key_rows), BF16),
            pltpu.VMEM((key_rows, HD), F32),
            pltpu.VMEM((-(-own_rows // QUERY_BLOCK), HD, GROUP * QUERY_BLOCK), BF16),
            pltpu.VMEM((-(-own_rows // QUERY_BLOCK) * QUERY_BLOCK, BACK), BF16),
            pltpu.VMEM((key_rows, GROUP * QUERY_BLOCK), F32),
            pltpu.SemaphoreType.DMA((spans,)),
        ],
        in_specs=[pl.BlockSpec(memory_space=pl.ANY)],
    )(got)


def local(query_rows, key_rows, value_rows, owner_ids):
    owners = lax.axis_size("seq")
    spans = lax.axis_size("span")
    row_count = query_rows.shape[1]
    rows = owners * TILE
    shape = jax.ShapeDtypeStruct
    send = call(
        pack_kernel,
        "pack",
        shape((KVH * rows, WIDE), BF16),
        4 * rows * row_count * HQ * HD,
        8 * rows * WIDE,
        [
            pltpu.VMEM((row_count, HQ * HD), BF16),
            pltpu.VMEM((row_count, KVH * HD), BF16),
            pltpu.VMEM((row_count, KVH * HD), BF16),
            pltpu.VMEM((KVH, rows, WIDE), BF16),
            pltpu.SemaphoreType.DMA((3,)),
            pltpu.SemaphoreType.DMA((KVH,)),
        ],
        limit=PACK_LIMIT,
        in_specs=[pl.BlockSpec(memory_space=pltpu.VMEM)] + [pl.BlockSpec(memory_space=pl.ANY)] * 3,
        out_specs=pl.BlockSpec(memory_space=pl.ANY),
    )(owner_ids, query_rows[0], key_rows[0], value_rows[0])
    got = exchange(send.reshape(KVH * owners, TILE, WIDE)).reshape(spans * rows, WIDE)
    done = attend(got, owners, spans)
    result = call(
        unpack_kernel,
        "unpack",
        shape((row_count, HQ * HD), BF16),
        2 * rows * row_count * HQ * HD,
        4 * rows * HQ * HD,
    )(owner_ids, exchange(done))
    return result[None]


def solution(mesh):
    return jax.shard_map(
        local,
        mesh=mesh,
        in_specs=(
            P("span", "seq", None),
            P("span", "seq", None),
            P("span", "seq", None),
            P("span", "seq"),
        ),
        out_specs=P("span", "seq", None),
        check_vma=False,
    )
```

```python
import functools
import math

import jax
import jax.numpy as jnp
from jax import lax
from jax.experimental import pallas as pl
from jax.experimental.pallas import tpu as pltpu
from jax.sharding import PartitionSpec as P

HQ = 24
KVH = 4
HD = 128
GROUP = HQ // KVH
TILE = 8
SLOTS = 7
WIDE = SLOTS * HD
BACK = GROUP * HD
FOUR = 4
LATE = SLOTS - FOUR
SIDE = (GROUP - 1) * HD
RETURNED = BACK + SIDE
KEY_BLOCK = 256
QUERY_BLOCK = 128
HALF_BLOCK = QUERY_BLOCK // 2
ALIGN = 16
EMPTY = 2.0**100
F32 = jnp.float32
BF16 = jnp.bfloat16
VMEM_LIMIT = 48 << 20
PACK_LIMIT = 58 << 20


def iota(shape, dim):
    return lax.broadcasted_iota(jnp.int32, shape, dim)


def row_ranks(owner_ref, axis):
    count = owner_ref.shape[1]
    along = jnp.broadcast_to(owner_ref[...].astype(F32), (count, count))
    down = along.T
    earlier = (along == down) & (iota((count, count), axis) < iota((count, count), 1 - axis))
    rank = jnp.sum(jnp.where(earlier, 1.0, 0.0), axis=axis, keepdims=True)
    owner = owner_ref[...] if axis == 0 else down[:, :1].astype(jnp.int32)
    return owner, rank.astype(jnp.int32)


def one_hot(condition):
    return jnp.where(condition, 1.0, 0.0).astype(BF16)


def pack_kernel(
    owner_ref, query_hbm, key_hbm, value_hbm, out_hbm, query_ref, key_ref, value_ref, out_ref, sem, out_sem
):
    pairs = ((value_hbm, value_ref), (key_hbm, key_ref), (query_hbm, query_ref))
    copies = [pltpu.make_async_copy(source, target, sem.at[i]) for i, (source, target) in enumerate(pairs)]
    for copy in copies:
        copy.start()
    owner, rank = row_ranks(owner_ref, 0)
    count = owner.shape[1]
    rows = out_ref.shape[1]
    place = iota((rows, count), 0)
    chosen = jnp.where(place == owner * TILE + rank, 1.0, 0.0)
    filled = jnp.sum(chosen, axis=1, keepdims=True)
    slot = (iota((rows, 1), 0) & (TILE - 1)) < SLOTS
    mark = jnp.where(slot & (filled == 0.0), F32(EMPTY), F32(0.0))
    select = chosen.astype(BF16)
    spare = place == owner * TILE + SLOTS
    copies[0].wait()
    tails = [
        jnp.dot(one_hot(spare & (rank == k)), value_ref[...], preferred_element_type=F32) for k in range(SLOTS)
    ]
    copies[1].wait()
    copies[2].wait()
    leaving = []
    for c in range(KVH):
        own = slice(c * HD, (c + 1) * HD)
        keys = jnp.dot(select, key_ref[:, own], preferred_element_type=F32)
        out_ref[c, :, :HD] = (keys + mark + tails[0][:, own]).astype(BF16)
        queries = jnp.dot(select, query_ref[:, c * BACK : (c + 1) * BACK], preferred_element_type=F32)
        rest = jnp.concatenate([tails[k][:, own] for k in range(1, SLOTS)], axis=1)
        out_ref[c, :, HD:] = (queries + rest).astype(BF16)
        leave = pltpu.make_async_copy(out_ref.at[c], out_hbm.at[pl.ds(c * rows, rows), :], out_sem.at[c])
        leave.start()
        leaving.append(leave)
    for leave in leaving:
        leave.wait()


def spread_tail(spare_rows):
    tiles = spare_rows.shape[0]
    sub = iota((tiles, TILE, HD), 1)
    tail = jnp.zeros((tiles, TILE, HD), F32)
    for k in range(SLOTS):
        piece = jnp.broadcast_to(spare_rows[:, :, k * HD : (k + 1) * HD], (tiles, TILE, HD))
        tail = jnp.where(sub == k, piece, tail)
    return tail.reshape(tiles * TILE, HD)


def returned_places(flags, first):
    rows = flags.shape[0]
    shape = (rows // TILE * FOUR, rows)
    line = iota(shape, 0)
    row = (line // FOUR) * TILE + (line & (FOUR - 1)) + first
    ahead = jnp.dot(one_hot(iota(shape, 1) < row), flags, preferred_element_type=F32)
    held = jnp.dot(one_hot(iota(shape, 1) == row), flags, preferred_element_type=F32)
    return jnp.where(held > 0.5, ahead, -1.0)


def picks(place, slots):
    wide = jnp.concatenate([place] * (slots // HD), axis=1)
    return one_hot(wide == iota(wide.shape, 1).astype(F32))


def attend_kernel(
    got_ref, out_ref, x_ref, before_ref, k_ref, v_ref, turned_ref, bias_ref, query_ref, held_ref, score_ref, sem
):
    spans = x_ref.shape[0]
    rows = x_ref.shape[1]
    blocks = query_ref.shape[0]
    factor = F32(math.log2(math.e) / math.sqrt(HD))

    def arrival(t):
        source = got_ref.at[pl.ds(pl.multiple_of(t * rows, rows), rows), :]
        return pltpu.make_async_copy(source, x_ref.at[t, :, pl.ds(0, WIDE)], sem.at[t])

    for t in range(spans):
        arrival(t).start()
    before_ref[...] = one_hot(iota((rows, rows), 1) < iota((rows, rows), 0))
    k_ref[...] = jnp.zeros_like(k_ref)
    v_ref[...] = jnp.zeros_like(v_ref)
    bias_ref[...] = jnp.full(bias_ref.shape, -1e30, F32)

    def span_step(t, offset):
        arrival(t).wait()
        spare_rows = x_ref[t, :, :WIDE].astype(F32).reshape(rows // TILE, TILE, WIDE)[:, SLOTS:, :]
        x_ref[t, :, WIDE:] = spread_tail(spare_rows).astype(BF16)
        marks = x_ref[t, :, :HD].astype(F32)
        valid = (marks < F32(EMPTY / 2)) & ((iota((rows, HD), 0) & (TILE - 1)) < SLOTS)
        ahead = jnp.dot(before_ref[...], one_hot(valid), preferred_element_type=F32)
        down = jnp.where(valid, ahead, -1.0)
        along = down.T[:1].astype(jnp.int32)
        total = (jnp.max(down) + 1.0).astype(jnp.int32)
        halves = (total + HALF_BLOCK - 1) // HALF_BLOCK
        count = halves // 2
        odd = halves % 2 == 1

        def gather_block(size, i):
            fold = one_hot(iota((size, rows), 0) + i * QUERY_BLOCK == along)
            dense = jnp.dot(fold, x_ref[t], preferred_element_type=F32)
            at = pl.ds(pl.multiple_of(offset + i * QUERY_BLOCK, ALIGN), size)
            k_ref[at, :] = dense[:, :HD].astype(BF16)
            v_ref[at, :] = dense[:, WIDE:]
            inside = iota((size, HD), 0) + i * QUERY_BLOCK < total
            bias_ref[at, :] = jnp.where(inside, F32(0.0), F32(-1e30))
            stack = jnp.concatenate([dense[:, (1 + h) * HD : (2 + h) * HD] for h in range(GROUP)], axis=0)
            query_ref[i, :, : GROUP * size] = stack.T.astype(BF16)

        def whole_block(i, _):
            gather_block(QUERY_BLOCK, i)
            return 0

        lax.fori_loop(0, count, whole_block, 0)
        pl.when(odd)(functools.partial(gather_block, HALF_BLOCK, count))
        end = offset + total

        def turn_block(b, _):
            at = pl.ds(pl.multiple_of(b * KEY_BLOCK, KEY_BLOCK), KEY_BLOCK)
            turned_ref[:, at] = v_ref[at, :].T.astype(BF16)
            return 0

        key_blocks = (end + KEY_BLOCK - 1) // KEY_BLOCK
        lax.fori_loop(offset // KEY_BLOCK, key_blocks, turn_block, 0)

        def attend_block(size, i, used):
            lanes = GROUP * size
            query = query_ref[i, :, :lanes]
            at = pl.ds(pl.multiple_of(i * QUERY_BLOCK, HALF_BLOCK), size)
            top = jnp.full((1, lanes), -1e30, F32)
            for b in range(0, used, 2):
                part = slice(b * KEY_BLOCK, min(b + 2, used) * KEY_BLOCK)
                bias = jnp.concatenate([bias_ref[part, :]] * (lanes // HD), axis=1)
                scores = jnp.dot(k_ref[part, :], query, preferred_element_type=F32) * factor + bias
                score_ref[part, :lanes] = scores
                top = jnp.maximum(top, jnp.max(scores, axis=0, keepdims=True))
            total = jnp.zeros((1, lanes), F32)
            accum = jnp.zeros((HD, lanes), F32)
            for b in range(0, used, 2):
                part = slice(b * KEY_BLOCK, min(b + 2, used) * KEY_BLOCK)
                weights = jnp.exp2(score_ref[part, :lanes] - top)
                total = total + jnp.sum(weights, axis=0, keepdims=True)
                accum = accum + jnp.dot(turned_ref[:, part], weights.astype(BF16), preferred_element_type=F32)
            result = (accum / total).T.astype(BF16)
            for h in range(GROUP):
                held_ref[at, h * HD : (h + 1) * HD] = result[h * size : (h + 1) * size]

        def by_keys(size, i):
            for used in range(1, turned_ref.shape[1] // KEY_BLOCK + 1):
                pl.when(key_blocks == used)(functools.partial(attend_block, size, i, used))

        def query_step(i, _):
            by_keys(QUERY_BLOCK, i)
            return 0

        lax.fori_loop(0, count, query_step, 0)
        pl.when(odd)(functools.partial(by_keys, HALF_BLOCK, count))

        def clear_block(i, _):
            at = pl.ds(pl.multiple_of(i * HALF_BLOCK, HALF_BLOCK), HALF_BLOCK)
            held_ref[at, :] = jnp.zeros((HALF_BLOCK, BACK), BF16)
            return 0

        lax.fori_loop(halves, blocks * QUERY_BLOCK // HALF_BLOCK, clear_block, 0)
        slots = blocks * QUERY_BLOCK
        flags = one_hot(valid)
        early = returned_places(flags, 0)
        late = returned_places(flags, FOUR)
        last = (iota((early.shape[0], HD), 0) & (FOUR - 1)) == FOUR - 1
        at = pl.ds(pl.multiple_of(t * (rows // TILE), rows // TILE), rows // TILE)
        moved = jnp.dot(picks(early, slots), held_ref[...], preferred_element_type=F32)
        out_ref[at, :, :BACK] = moved.astype(BF16).reshape(rows // TILE, FOUR, BACK)
        moved = jnp.dot(picks(late, slots), held_ref[...], preferred_element_type=F32)
        sixth = moved[:, SIDE:]
        for j in range(GROUP - 1):
            piece = moved[:, j * HD : (j + 1) * HD]
            if j < LATE:
                piece = jnp.where(last, pltpu.roll(sixth, FOUR - 1 - j, 0), piece)
            lane = BACK + j * HD
            out_ref[at, :, lane : lane + HD] = piece.astype(BF16).reshape(rows // TILE, FOUR, HD)
        return offset + (total + ALIGN - 1) // ALIGN * ALIGN

    lax.fori_loop(0, spans, span_step, jnp.int32(0))


def unpack_kernel(owner_ref, got_ref, out_ref):
    owner, rank = row_ranks(owner_ref, 1)
    count = owner.shape[0]
    owners = got_ref.shape[0] // KVH
    lines = owners * FOUR
    line = iota((count, lines), 1)
    early = one_hot((line == owner * FOUR + rank) & (rank < FOUR))
    late = one_hot((line == owner * FOUR + rank - FOUR) & (rank >= FOUR))
    aside = line == owner * FOUR + FOUR - 1
    for c in range(KVH):
        part = got_ref[c * owners : (c + 1) * owners].reshape(lines, RETURNED)
        moved = jnp.dot(early, part[:, :BACK], preferred_element_type=F32)
        more = jnp.dot(late, part[:, BACK:], preferred_element_type=F32)
        out_ref[:, c * BACK : c * BACK + SIDE] = (moved[:, :SIDE] + more).astype(BF16)
        sixth = moved[:, SIDE:]
        for s in range(LATE):
            lane = BACK + s * HD
            chosen = one_hot(aside & (rank == FOUR + s))
            sixth = sixth + jnp.dot(chosen, part[:, lane : lane + HD], preferred_element_type=F32)
        out_ref[:, c * BACK + SIDE : (c + 1) * BACK] = sixth.astype(BF16)


def call(kernel, name, out_shape, flops, moved, scratch=(), limit=VMEM_LIMIT, **specs):
    return pl.pallas_call(
        kernel,
        out_shape=out_shape,
        scratch_shapes=list(scratch),
        compiler_params=pltpu.CompilerParams(vmem_limit_bytes=limit),
        cost_estimate=pl.CostEstimate(flops=flops, bytes_accessed=moved, transcendentals=0),
        name=name,
        **specs,
    )


def exchange(chunks):
    return lax.all_to_all(chunks, ("span", "seq"), split_axis=0, concat_axis=0, tiled=True)


def attend(got, owners, spans):
    rows = owners * TILE
    own_rows = owners * SLOTS
    key_blocks = -(-(spans * own_rows + QUERY_BLOCK) // KEY_BLOCK)
    key_rows = key_blocks * KEY_BLOCK
    return call(
        attend_kernel,
        "attend",
        jax.ShapeDtypeStruct((spans * owners, FOUR, RETURNED), BF16),
        4 * own_rows * own_rows * spans * spans * HD * GROUP,
        4 * spans * rows * WIDE,
        [
            pltpu.VMEM((spans, rows, WIDE + HD), BF16),
            pltpu.VMEM((rows, rows), BF16),
            pltpu.VMEM((key_rows, HD), BF16),
            pltpu.VMEM((key_rows, HD), F32),
            pltpu.VMEM((HD, key_rows), BF16),
            pltpu.VMEM((key_rows, HD), F32),
            pltpu.VMEM((-(-own_rows // QUERY_BLOCK), HD, GROUP * QUERY_BLOCK), BF16),
            pltpu.VMEM((-(-own_rows // QUERY_BLOCK) * QUERY_BLOCK, BACK), BF16),
            pltpu.VMEM((key_rows, GROUP * QUERY_BLOCK), F32),
            pltpu.SemaphoreType.DMA((spans,)),
        ],
        in_specs=[pl.BlockSpec(memory_space=pl.ANY)],
    )(got)


def local(query_rows, key_rows, value_rows, owner_ids):
    owners = lax.axis_size("seq")
    spans = lax.axis_size("span")
    row_count = query_rows.shape[1]
    rows = owners * TILE
    shape = jax.ShapeDtypeStruct
    send = call(
        pack_kernel,
        "pack",
        shape((KVH * rows, WIDE), BF16),
        4 * rows * row_count * HQ * HD,
        8 * rows * WIDE,
        [
            pltpu.VMEM((row_count, HQ * HD), BF16),
            pltpu.VMEM((row_count, KVH * HD), BF16),
            pltpu.VMEM((row_count, KVH * HD), BF16),
            pltpu.VMEM((KVH, rows, WIDE), BF16),
            pltpu.SemaphoreType.DMA((3,)),
            pltpu.SemaphoreType.DMA((KVH,)),
        ],
        limit=PACK_LIMIT,
        in_specs=[pl.BlockSpec(memory_space=pltpu.VMEM)] + [pl.BlockSpec(memory_space=pl.ANY)] * 3,
        out_specs=pl.BlockSpec(memory_space=pl.ANY),
    )(owner_ids, query_rows[0], key_rows[0], value_rows[0])
    got = exchange(send.reshape(KVH * owners, TILE, WIDE)).reshape(spans * rows, WIDE)
    done = attend(got, owners, spans)
    result = call(
        unpack_kernel,
        "unpack",
        shape((row_count, HQ * HD), BF16),
        2 * rows * row_count * HQ * HD,
        4 * rows * HQ * HD,
    )(owner_ids, exchange(done))
    return result[None]


def solution(mesh):
    return jax.shard_map(
        local,
        mesh=mesh,
        in_specs=(
            P("span", "seq", None),
            P("span", "seq", None),
            P("span", "seq", None),
            P("span", "seq"),
        ),
        out_specs=P("span", "seq", None),
        check_vma=False,
    )
```
